128 devices in a mesh: shard: 16 (over y, x), rep: 8 (over z, core).
Axes of the slice: x: 4, y: 4, z: 4, core: 2. Of those that a mesh axis runs over, the one named last changes fastest.
Arguments:
- tokens: bfloat16 [18432, 1024], P(('shard', 'rep')), may hold values from -6 to 6
- positions: int32 [18432], P(('shard', 'rep')), may hold values from 0 to 143, as said below
- cotangent: bfloat16 [18432, 1024], P(('shard', 'rep')), may hold values from -6 to 6
- attn_gain: bfloat16 [1024], P('shard'), may hold values from 0.5 to 1.5
- w_query: bfloat16 [1024, 2048], P('shard'), may hold values from -0.1875 to 0.1875
- key_projection: bfloat16 [1024, 1024], P('shard'), may hold values from -0.1875 to 0.1875
- value_projection: bfloat16 [1024, 1024], P('shard'), may hold values from -0.1875 to 0.1875
- q_gain: bfloat16 [128], P('shard'), may hold values from 0.5 to 1.5
- k_gain: bfloat16 [128], P('shard'), may hold values from 0.5 to 1.5
- w_output: bfloat16 [2048, 1024], P('shard'), may hold values from -0.5 to 0.5
- ffn_gain: bfloat16 [1024], P('shard'), may hold values from 0.5 to 1.5
- w_gate: bfloat16 [1024, 3072], P('shard'), may hold values from -0.1875 to 0.1875
- w_up: bfloat16 [1024, 3072], P('shard'), may hold values from -0.1875 to 0.1875
- w_down: bfloat16 [3072, 1024], P('shard'), may hold values from -0.109375 to 0.109375
Outputs:
- mixed: bfloat16 [18432, 1024], P(('shard', 'rep'))
- grad_tokens: bfloat16 [18432, 1024], P(('shard', 'rep'))
- grad_attn_gain: float32 [1024], P('shard')
- grad_query: float32 [1024, 2048], P('shard')
- grad_key: float32 [1024, 1024], P('shard')
- grad_value: float32 [1024, 1024], P('shard')
- grad_q_gain: float32 [128], P('shard')
- grad_k_gain: float32 [128], P('shard')
- grad_output: float32 [2048, 1024], P('shard')
- grad_ffn_gain: float32 [1024], P('shard')
- grad_gate: float32 [1024, 3072], P('shard')
- grad_up: float32 [1024, 3072], P('shard')
- grad_down: float32 [3072, 1024], P('shard')
The draws below stay inside these ranges and needn't reach their ends.
Inputs may be any that keep to these rules, and one draw needn't show every extreme that they name: `positions`: within each aligned block of 144 tokens, the first token has position 0 and every other token has its predecessor's position plus one, or 0 where a packed document starts.
All inputs are finite; a program needn't handle non-finite values.
Results may differ from the reference program's by a relative error of at most 0.03.
Values may be sent and summed in bfloat16 or wider, within the bound.
No kernel may reach another device: no remote copies, remote signals or barrier semaphores. Data moves between devices by JAX's collectives and lax.ppermute only.
A program may use at most 192 MiB of HBM per device.

```python
import math
import jax
import jax.numpy as jnp
from jax import lax

MODEL_WIDTH = 1024
HQ = 16
KEY_VALUE_HEADS = 8
HEAD_SIZE = 128
FF = 3072
TOK_DEV = 144
TOKENS = 18432


def draw_positions(key, part):
    blocks = TOKENS // TOK_DEV
    first_key = jax.random.fold_in(key, 11)
    second_key = jax.random.fold_in(key, 12)
    boundary = jax.random.randint(first_key, (blocks, TOK_DEV), 0, 24) == 0
    columns = jnp.arange(TOK_DEV, dtype=jnp.int32)
    chosen = jax.random.randint(second_key, (), 0, blocks)
    whole_rows = jnp.arange(blocks, dtype=jnp.int32)[:, None] == chosen
    boundary = jnp.where(columns[None, :] == 0, True, jnp.where(whole_rows, False, boundary))
    starts = jnp.where(boundary, columns[None, :], 0)
    latest = lax.cummax(starts, axis=1)
    return (columns[None, :] - latest).reshape(TOKENS).astype(jnp.int32)


def steps_of(stream_key, extent, cuts, low, top_value):
    level, own = 1.0, jax.random.fold_in(stream_key, 6)
    for position, parts in cuts:
        draws = jnp.exp(jax.random.uniform(jax.random.fold_in(own, position), (parts,), jnp.float32, low / len(cuts), top_value / len(cuts)))
        level = level * jnp.repeat(draws, extent[position] // parts).reshape([-1 if axis == position else 1 for axis in range(len(extent))])
    return level


def centred(rng, extent, width, limit, cuts=(), held_as=jnp.bfloat16):
    factor_of = steps_of(rng, extent, cuts, -0.22, 0.18) if cuts else 1.0
    drawn = jax.random.normal(rng, extent, jnp.float32) * width * factor_of
    return jnp.minimum(jnp.maximum(drawn, -limit), limit).astype(held_as)


def setup_inputs(seed: int = 0) -> dict:
    arg_keys = jax.random.split(jax.random.key(seed), 15)
    return {
        "tokens": centred(arg_keys[0], (TOKENS, MODEL_WIDTH), 1.0, 6.0, ((0, 128),)),
        "positions": draw_positions(jax.random.fold_in(arg_keys[14], 71), 0),
        "cotangent": centred(arg_keys[2], (TOKENS, MODEL_WIDTH), 1.0, 6.0, ((0, 128),)),
        "attn_gain": jnp.clip(1.0 + 0.1 * jax.random.normal(arg_keys[3], (MODEL_WIDTH,), jnp.float32), 0.5, 1.5).astype(jnp.bfloat16),
        "w_query": centred(arg_keys[4], (MODEL_WIDTH, HQ * HEAD_SIZE), MODEL_WIDTH ** -0.5, 0.1875, ((0, 16),)),
        "key_projection": centred(arg_keys[5], (MODEL_WIDTH, KEY_VALUE_HEADS * HEAD_SIZE), MODEL_WIDTH ** -0.5, 0.1875, ((0, 16),)),
        "value_projection": centred(arg_keys[6], (MODEL_WIDTH, KEY_VALUE_HEADS * HEAD_SIZE), MODEL_WIDTH ** -0.5, 0.1875, ((0, 16),)),
        "q_gain": jnp.clip(1.0 + 0.1 * jax.random.normal(arg_keys[7], (HEAD_SIZE,), jnp.float32), 0.5, 1.5).astype(jnp.bfloat16),
        "k_gain": jnp.clip(1.0 + 0.1 * jax.random.normal(arg_keys[8], (HEAD_SIZE,), jnp.float32), 0.5, 1.5).astype(jnp.bfloat16),
        "w_output": centred(arg_keys[9], (HQ * HEAD_SIZE, MODEL_WIDTH), (HQ * HEAD_SIZE // 16) ** -0.5, 0.5, ((0, 16),)),
        "ffn_gain": jnp.clip(1.0 + 0.1 * jax.random.normal(arg_keys[10], (MODEL_WIDTH,), jnp.float32), 0.5, 1.5).astype(jnp.bfloat16),
        "w_gate": centred(arg_keys[11], (MODEL_WIDTH, FF), MODEL_WIDTH ** -0.5, 0.1875, ((0, 16),)),
        "w_up": centred(arg_keys[12], (MODEL_WIDTH, FF), MODEL_WIDTH ** -0.5, 0.1875, ((0, 16),)),
        "w_down": centred(arg_keys[13], (FF, MODEL_WIDTH), FF ** -0.5, 0.109375, ((0, 16),)),
    }


EPSILON = 1e-06
THETA = 1000000.0

def rms_forward(inputs, scales):
    factor = lax.rsqrt(lax.optimization_barrier(jnp.mean(inputs * inputs, axis=-1, keepdims=True)) + EPSILON)
    normed = inputs * factor
    return (normed * scales, normed, factor)

def rms_backward(grad_out, scales, normed, factor):
    grad_normed = grad_out * scales
    grad_in = factor * (grad_normed - normed * lax.optimization_barrier(jnp.mean(grad_normed * normed, axis=-1, keepdims=True)))
    lead_axes = tuple(range(grad_out.ndim - 1))
    return (grad_in, lax.optimization_barrier(jnp.sum(grad_out * normed, axis=lead_axes)))

def rope_tables(positions, head_dim):
    half_dim = head_dim // 2
    frequency = jnp.exp(jnp.arange(half_dim).astype(jnp.float32) * (-2.0 * math.log(THETA) / head_dim))
    angles = positions.astype(jnp.float32)[:, None] * frequency[None, :]
    return (jnp.cos(angles)[:, None, :], jnp.sin(angles)[:, None, :])

def rotate(inputs, cosine_lookup, sine_lookup):
    half_dim = inputs.shape[-1] // 2
    first_half = inputs[..., :half_dim]
    second_half = inputs[..., half_dim:]
    return jnp.concatenate([first_half * cosine_lookup - second_half * sine_lookup, second_half * cosine_lookup + first_half * sine_lookup], axis=-1)

def inverse_rotation(grad_out, cosine_lookup, sine_lookup):
    half_dim = grad_out.shape[-1] // 2
    first_half = grad_out[..., :half_dim]
    second_half = grad_out[..., half_dim:]
    return jnp.concatenate([first_half * cosine_lookup + second_half * sine_lookup, second_half * cosine_lookup - first_half * sine_lookup], axis=-1)

def allowed_mask(positions):
    row_index = jnp.arange(positions.shape[0], dtype=jnp.int32)
    starts = row_index - positions.astype(jnp.int32)
    return (row_index[None, :] <= row_index[:, None]) & (row_index[None, :] >= starts[:, None])

def to_float(low_value):
    return lax.optimization_barrier(low_value).astype(jnp.float32)

def block_scores(queries, key_rows, positions):
    length, head_count, head_dim = queries.shape
    kv_heads = key_rows.shape[1]
    grouped = queries.reshape(length, kv_heads, head_count // kv_heads, head_dim).astype(jnp.float32)
    scores = jnp.einsum('qhgd,khd->hgqk', grouped, key_rows.astype(jnp.float32)) * head_dim ** (-0.5)
    return jnp.where(allowed_mask(positions)[None, None], scores, -1e+30)

def block_forward(queries, key_rows, value_rows, positions):
    length, head_count, head_dim = queries.shape
    scores = block_scores(queries, key_rows, positions)
    row_peak = lax.optimization_barrier(jnp.max(scores, axis=-1, keepdims=True))
    weights = jnp.exp(scores - row_peak)
    row_total = lax.optimization_barrier(jnp.sum(weights, axis=-1, keepdims=True))
    prob_low = (weights / row_total).astype(jnp.bfloat16)
    attended = jnp.einsum('hgqk,khd->qhgd', to_float(prob_low), value_rows.astype(jnp.float32))
    log_total = (row_peak + jnp.log(row_total))[..., 0]
    return (attended.reshape(length, head_count * head_dim), log_total)

def block_backward(queries, key_rows, value_rows, positions, log_total, grad_attended, attended_low):
    length, head_count, head_dim = queries.shape
    kv_heads = key_rows.shape[1]
    groups = head_count // kv_heads
    scores = block_scores(queries, key_rows, positions)
    probability = jnp.exp(scores - log_total[..., None])
    prob_low = probability.astype(jnp.bfloat16)
    grad_grouped = grad_attended.reshape(length, kv_heads, groups, head_dim).astype(jnp.float32)
    attended_grouped = attended_low.reshape(length, kv_heads, groups, head_dim).astype(jnp.float32)
    value_gradient_rows = jnp.einsum('hgqk,qhgd->khd', to_float(prob_low), grad_grouped)
    grad_probs = jnp.einsum('qhgd,khd->hgqk', grad_grouped, value_rows.astype(jnp.float32))
    row_delta = jnp.transpose(lax.optimization_barrier(jnp.sum(grad_grouped * attended_grouped, axis=-1)), (1, 2, 0))
    grad_scores = (probability * (grad_probs - row_delta[..., None]) * head_dim ** (-0.5)).astype(jnp.bfloat16)
    scores_float = to_float(grad_scores)
    grouped = queries.reshape(length, kv_heads, groups, head_dim).astype(jnp.float32)
    grad_query_rows = jnp.einsum('hgqk,khd->qhgd', scores_float, key_rows.astype(jnp.float32)).reshape(length, head_count, head_dim)
    grad_key_rows = jnp.einsum('hgqk,qhgd->khd', scores_float, grouped)
    return (grad_query_rows, grad_key_rows, value_gradient_rows)

def matrix_product(left, right):
    return jnp.dot(left, right, preferred_element_type=jnp.float32)

def reference(tokens, positions, cotangent, attn_gain, w_query, key_projection, value_projection, q_gain, k_gain, w_output, ffn_gain, w_gate, w_up, w_down):
    group_count = TOKENS // TOK_DEV
    replica_group_rows = TOK_DEV
    norm_one = attn_gain.astype(jnp.float32)
    norm_two = ffn_gain.astype(jnp.float32)
    query_scale = q_gain.astype(jnp.float32)
    key_scale = k_gain.astype(jnp.float32)

    def group_step(running, group_data):
        token_rows, position_rows, cotangent_rows = group_data
        stream_in = token_rows.astype(jnp.float32)
        first_out, first_unit, first_factor = rms_forward(stream_in, norm_one)
        first_reduced = first_out.astype(jnp.bfloat16)
        query_raw = matrix_product(first_reduced, w_query).reshape(replica_group_rows, HQ, HEAD_SIZE)
        key_unscaled = matrix_product(first_reduced, key_projection).reshape(replica_group_rows, KEY_VALUE_HEADS, HEAD_SIZE)
        value_reduced = matrix_product(first_reduced, value_projection).astype(jnp.bfloat16).reshape(replica_group_rows, KEY_VALUE_HEADS, HEAD_SIZE)
        query_normed, query_unit, query_factor = rms_forward(query_raw, query_scale)
        key_normed, key_unit, key_factor = rms_forward(key_unscaled, key_scale)
        cosine_lookup, sine_lookup = rope_tables(position_rows, HEAD_SIZE)
        query_low = rotate(query_normed, cosine_lookup, sine_lookup).astype(jnp.bfloat16)
        key_low = rotate(key_normed, cosine_lookup, sine_lookup).astype(jnp.bfloat16)
        attended, log_total = block_forward(query_low, key_low, value_reduced, position_rows)
        attended_low = attended.reshape(replica_group_rows, HQ * HEAD_SIZE).astype(jnp.bfloat16)
        middle = stream_in + matrix_product(attended_low, w_output)
        second_out, second_unit, second_factor = rms_forward(middle, norm_two)
        second_low = second_out.astype(jnp.bfloat16)
        gate_value = matrix_product(second_low, w_gate)
        upper_value = matrix_product(second_low, w_up)
        sigmoid_gate = jax.nn.sigmoid(gate_value)
        hidden_low = (gate_value * sigmoid_gate * upper_value).astype(jnp.bfloat16)
        mixed = (middle + matrix_product(hidden_low, w_down)).astype(jnp.bfloat16)
        grad_down = matrix_product(hidden_low.T, cotangent_rows)
        grad_hidden = matrix_product(cotangent_rows, w_down.T)
        grad_gate_low = (grad_hidden * upper_value * sigmoid_gate * (1.0 + gate_value * (1.0 - sigmoid_gate))).astype(jnp.bfloat16)
        grad_upper_low = (grad_hidden * gate_value * sigmoid_gate).astype(jnp.bfloat16)
        grad_gate = matrix_product(second_low.T, grad_gate_low)
        grad_upper = matrix_product(second_low.T, grad_upper_low)
        grad_second = matrix_product(grad_gate_low, w_gate.T) + matrix_product(grad_upper_low, w_up.T)
        grad_middle_part, grad_norm_two = rms_backward(grad_second, norm_two, second_unit, second_factor)
        grad_middle = cotangent_rows.astype(jnp.float32) + grad_middle_part
        grad_middle_low = grad_middle.astype(jnp.bfloat16)
        grad_output = matrix_product(attended_low.T, grad_middle_low)
        grad_attended_low = matrix_product(grad_middle_low, w_output.T).astype(jnp.bfloat16)
        grad_query_rot, key_gradient_rotated, value_gradient_rows = block_backward(query_low, key_low, value_reduced, position_rows, log_total, grad_attended_low, attended_low)
        grad_query_normed = inverse_rotation(grad_query_rot.reshape(replica_group_rows, HQ, HEAD_SIZE), cosine_lookup, sine_lookup)
        key_gradient_normalized = inverse_rotation(key_gradient_rotated.reshape(replica_group_rows, KEY_VALUE_HEADS, HEAD_SIZE), cosine_lookup, sine_lookup)
        grad_query_raw, grad_query_scale = rms_backward(grad_query_normed, query_scale, query_unit, query_factor)
        key_gradient_unscaled, grad_key_scale = rms_backward(key_gradient_normalized, key_scale, key_unit, key_factor)
        grad_query_low = grad_query_raw.reshape(replica_group_rows, HQ * HEAD_SIZE).astype(jnp.bfloat16)
        key_gradient_reduced = key_gradient_unscaled.reshape(replica_group_rows, KEY_VALUE_HEADS * HEAD_SIZE).astype(jnp.bfloat16)
        value_gradient_reduced = value_gradient_rows.reshape(replica_group_rows, KEY_VALUE_HEADS * HEAD_SIZE).astype(jnp.bfloat16)
        grad_query_weight = matrix_product(first_reduced.T, grad_query_low)
        grad_key_weight = matrix_product(first_reduced.T, key_gradient_reduced)
        grad_value_weight = matrix_product(first_reduced.T, value_gradient_reduced)
        grad_first = matrix_product(grad_query_low, w_query.T) + matrix_product(key_gradient_reduced, key_projection.T) + matrix_product(value_gradient_reduced, value_projection.T)
        grad_in_part, grad_norm_one = rms_backward(grad_first, norm_one, first_unit, first_factor)
        grad_tokens = (grad_middle + grad_in_part).astype(jnp.bfloat16)
        updates = (grad_norm_one, grad_query_weight, grad_key_weight, grad_value_weight, grad_query_scale, grad_key_scale, grad_output, grad_norm_two, grad_gate, grad_upper, grad_down)
        summed = tuple((older + to_float(newer.astype(jnp.bfloat16)) for older, newer in zip(running, updates)))
        return (summed, (mixed, grad_tokens))
    starting = (jnp.zeros(attn_gain.shape, jnp.float32), jnp.zeros(w_query.shape, jnp.float32), jnp.zeros(key_projection.shape, jnp.float32), jnp.zeros(value_projection.shape, jnp.float32), jnp.zeros(q_gain.shape, jnp.float32), jnp.zeros(k_gain.shape, jnp.float32), jnp.zeros(w_output.shape, jnp.float32), jnp.zeros(ffn_gain.shape, jnp.float32), jnp.zeros(w_gate.shape, jnp.float32), jnp.zeros(w_up.shape, jnp.float32), jnp.zeros(w_down.shape, jnp.float32))
    sliced = (tokens.reshape(group_count, replica_group_rows, MODEL_WIDTH), positions.reshape(group_count, replica_group_rows), cotangent.reshape(group_count, replica_group_rows, MODEL_WIDTH))
    totals, (mixed_all, grad_all) = lax.scan(group_step, starting, sliced)
    return (mixed_all.reshape(TOKENS, MODEL_WIDTH), grad_all.reshape(TOKENS, MODEL_WIDTH), totals[0], totals[1], totals[2], totals[3], totals[4], totals[5], totals[6], totals[7], totals[8], totals[9], totals[10])
```

```python
import math

import jax
import jax.numpy as jnp
from jax import lax
from jax.sharding import Mesh, PartitionSpec as P

EPSILON = 1e-06
THETA = 1000000.0
SHARD = ("y", "x")
REP = ("z", "c")
NS = 16
NR = 8
BF = jnp.bfloat16
F32 = jnp.float32


def rms_forward(inputs, scales):
    factor = lax.rsqrt(jnp.mean(inputs * inputs, axis=-1, keepdims=True) + EPSILON)
    normed = inputs * factor
    return (normed * scales, normed, factor)


def rms_backward(grad_out, scales, normed, factor):
    grad_normed = grad_out * scales
    grad_in = factor * (
        grad_normed - normed * jnp.mean(grad_normed * normed, axis=-1, keepdims=True)
    )
    return (grad_in, jnp.sum(grad_out * normed, axis=tuple(range(grad_out.ndim - 1))))


def rope_tables(positions, head_dim):
    half_dim = head_dim // 2
    frequency = jnp.exp(
        jnp.arange(half_dim).astype(F32) * (-2.0 * math.log(THETA) / head_dim)
    )
    angles = positions.astype(F32)[..., None] * frequency
    return (jnp.cos(angles), jnp.sin(angles))


def rotate(inputs, cosine, sine):
    a, b = jnp.split(inputs, 2, axis=-1)
    return jnp.concatenate([a * cosine - b * sine, b * cosine + a * sine], axis=-1)


def inverse_rotation(grad_out, cosine, sine):
    a, b = jnp.split(grad_out, 2, axis=-1)
    return jnp.concatenate([a * cosine + b * sine, b * cosine - a * sine], axis=-1)


def mm(left, right):
    return jnp.dot(left, right, preferred_element_type=F32)


def mm_nt(left, right):
    return lax.dot_general(left, right, (((1,), (1,)), ((), ())), preferred_element_type=F32)


def mm_tn(left, right):
    return lax.dot_general(left, right, (((0,), (0,)), ((), ())), preferred_element_type=F32)


def spread(a, axes, n):
    return lax.all_to_all(jnp.broadcast_to(a[None], (n,) + a.shape), axes, 0, 0)


def gather_rep(a):
    return lax.all_gather(a, REP, axis=0, tiled=True)


def scatter_rep(a):
    n = a.shape[1]
    a = a.astype(BF).reshape(4, 2, a.shape[0] // 8, n)
    core = lax.axis_index("c")
    mine = lax.dynamic_index_in_dim(a, core, 1, False)
    other = lax.dynamic_index_in_dim(a, 1 - core, 1, False)
    got = lax.ppermute(other, "c", [(0, 1), (1, 0)])
    both = (mine.astype(F32) + got.astype(F32)).astype(BF)
    return lax.all_to_all(both, "z", 0, 0).astype(F32).sum(0)


def scatter_shard(a):
    return lax.all_to_all(a.astype(BF), SHARD, 0, 0).astype(F32).sum(0)


def local(
    tokens,
    positions,
    cotangent,
    attn_gain,
    w_query,
    key_projection,
    value_projection,
    q_gain,
    k_gain,
    w_output,
    ffn_gain,
    w_gate,
    w_up,
    w_down,
):
    rep = 2 * lax.axis_index("z") + lax.axis_index("c")
    rows = tokens.shape[0]
    width = tokens.shape[1]
    head = 128
    cut = lambda w, n: lax.dynamic_slice_in_dim(w, rep * n, n, 1)
    cut_rows = lambda w, n: lax.dynamic_slice_in_dim(w, rep * n, n, 0)

    gains = jnp.concatenate(
        [attn_gain, ffn_gain, q_gain, k_gain, jnp.zeros((112,), BF)]
    ).reshape(2, 128)
    gains = spread(gains, SHARD, NS).reshape(NS, 256)
    norm_one = gains[:, :64].reshape(-1).astype(F32)
    norm_two = gains[:, 64:128].reshape(-1).astype(F32)
    q_scale = gains[:, 128:136].reshape(-1).astype(F32)
    k_scale = gains[:, 136:144].reshape(-1).astype(F32)

    w_in = jnp.concatenate(
        [cut(w_query, 256), cut(key_projection, 128), cut(value_projection, 128)], axis=1
    )
    w_in = spread(w_in, SHARD, NS).reshape(width, 512)
    w_rows = jnp.concatenate([cut_rows(w_output, 16), cut_rows(w_down, 24)], axis=0)
    w_rows = lax.all_gather(w_rows, SHARD, axis=0)
    w_rows = lax.all_to_all(w_rows.reshape(NR, 2, 40, width), REP, 0, 0)
    w_out = jnp.transpose(w_rows[:, :, :16], (1, 0, 2, 3)).reshape(256, width)
    w_dn = jnp.transpose(w_rows[:, :, 16:], (1, 0, 2, 3)).reshape(384, width)
    w_ff = jnp.concatenate([cut(w_gate, 384), cut(w_up, 384)], axis=1)
    w_ff = lax.all_gather(w_ff, SHARD, axis=0, tiled=True)

    pos = gather_rep(positions.reshape(1, rows))
    cosine, sine = rope_tables(pos, head)

    stream_in = tokens.astype(F32)
    first_out, first_unit, first_factor = rms_forward(stream_in, norm_one)
    x1 = gather_rep(first_out.astype(BF))
    cot = gather_rep(cotangent)

    raw = mm(x1, w_in)
    q_raw = raw[:, :256].reshape(NR, rows, 2, head)
    k_raw = raw[:, 256:384].reshape(NR, rows, head)
    value = raw[:, 384:].astype(BF).reshape(NR, rows, head)
    q_normed, q_unit, q_factor = rms_forward(q_raw, q_scale)
    k_normed, k_unit, k_factor = rms_forward(k_raw, k_scale)
    query = rotate(q_normed, cosine[:, :, None], sine[:, :, None]).astype(BF)
    key = rotate(k_normed, cosine, sine).astype(BF)

    index = jnp.arange(rows, dtype=jnp.int32)
    starts = index[None, :] - pos
    mask = (index[None, None, :] <= index[None, :, None]) & (
        index[None, None, :] >= starts[:, :, None]
    )
    scores = jnp.einsum("bqhd,bkd->bhqk", query, key, preferred_element_type=F32)
    scores = jnp.where(mask[:, None], scores * head ** (-0.5), -1e30)
    peak = jnp.max(scores, axis=-1, keepdims=True)
    weights = jnp.exp(scores - peak)
    probability = weights / jnp.sum(weights, axis=-1, keepdims=True)
    prob_low = probability.astype(BF)
    attended = jnp.einsum("bhqk,bkd->bqhd", prob_low, value, preferred_element_type=F32)
    attended = attended.astype(BF)
    att = attended.reshape(NR * rows, 256)

    middle = stream_in + scatter_rep(mm(att, w_out))
    second_out, second_unit, second_factor = rms_forward(middle, norm_two)
    x2 = gather_rep(second_out.astype(BF))

    both = mm(x2, w_ff)
    gate, upper = both[:, :384], both[:, 384:]
    sig = jax.nn.sigmoid(gate)
    hidden = (gate * sig * upper).astype(BF)
    mixed = (middle + scatter_rep(mm(hidden, w_dn))).astype(BF)

    grad_hidden = mm_nt(cot, w_dn)
    grad_gate_low = (grad_hidden * upper * sig * (1.0 + gate * (1.0 - sig))).astype(BF)
    grad_upper_low = (grad_hidden * gate * sig).astype(BF)
    grad_both = jnp.concatenate([grad_gate_low, grad_upper_low], axis=1)
    grad_second = scatter_rep(mm_nt(grad_both, w_ff))
    g_ff = mm_tn(x2, grad_both)
    g_dn = mm_tn(hidden, cot)
    grad_part, g_norm_two = rms_backward(grad_second, norm_two, second_unit, second_factor)
    grad_middle = cotangent.astype(F32) + grad_part
    gm = gather_rep(grad_middle.astype(BF))

    g_out = mm_tn(att, gm)
    grad_att = mm_nt(gm, w_out).astype(BF).reshape(NR, rows, 2, head)
    grad_value = jnp.einsum("bhqk,bqhd->bkd", prob_low, grad_att, preferred_element_type=F32)
    grad_probs = jnp.einsum("bqhd,bkd->bhqk", grad_att, value, preferred_element_type=F32)
    delta = jnp.sum(grad_att.astype(F32) * attended.astype(F32), axis=-1)
    grad_scores = (
        probability * (grad_probs - jnp.transpose(delta, (0, 2, 1))[..., None]) * head ** (-0.5)
    ).astype(BF)
    grad_query = jnp.einsum("bhqk,bkd->bqhd", grad_scores, key, preferred_element_type=F32)
    grad_key = jnp.einsum("bhqk,bqhd->bkd", grad_scores, query, preferred_element_type=F32)
    grad_query, g_q = rms_backward(
        inverse_rotation(grad_query, cosine[:, :, None], sine[:, :, None]),
        q_scale, q_unit, q_factor,
    )
    grad_key, g_k = rms_backward(
        inverse_rotation(grad_key, cosine, sine), k_scale, k_unit, k_factor
    )
    tall = NR * rows
    grad_in = jnp.concatenate(
        [
            grad_query.astype(BF).reshape(tall, 256),
            grad_key.astype(BF).reshape(tall, 128),
            grad_value.astype(BF).reshape(tall, 128),
        ],
        axis=1,
    )
    grad_first = scatter_rep(mm_nt(grad_in, w_in))
    g_in = mm_tn(x1, grad_in)
    grad_part, g_norm_one = rms_backward(grad_first, norm_one, first_unit, first_factor)
    grad_tokens = (grad_middle + grad_part).astype(BF)

    g_ff = scatter_shard(g_ff.reshape(NS, 64, 768))
    g_in = scatter_shard(g_in.reshape(NS, 64, 512))
    g_rows = jnp.concatenate(
        [
            jnp.transpose(g_out.astype(BF).reshape(2, NR, 16, width), (1, 0, 2, 3)),
            jnp.transpose(g_dn.astype(BF).reshape(2, NR, 24, width), (1, 0, 2, 3)),
        ],
        axis=2,
    )
    g_rows = lax.all_to_all(g_rows, REP, 0, 0).reshape(NS, 40, width)
    g_rows = scatter_shard(g_rows)
    small = jnp.concatenate(
        [
            g_norm_one.reshape(NS, 64),
            g_norm_two.reshape(NS, 64),
            g_q.reshape(NS, 8),
            g_k.reshape(NS, 8),
            jnp.zeros((NS, 112), F32),
        ],
        axis=1,
    )
    small = scatter_shard(small.reshape(NS, 2, 128))
    small = spread(small.astype(BF), REP, NR).astype(F32).sum(0).reshape(256)

    g_ff = lax.all_gather(g_ff.astype(BF), REP, axis=0)
    g_in = lax.all_gather(g_in.astype(BF), REP, axis=0)
    g_rows = lax.all_gather(g_rows.astype(BF), REP, axis=0).astype(F32)
    wide = lambda g: jnp.transpose(g.astype(F32), (1, 0, 2)).reshape(64, -1)
    return (
        mixed,
        grad_tokens,
        small[:64],
        wide(g_in[:, :, :256]),
        wide(g_in[:, :, 256:384]),
        wide(g_in[:, :, 384:]),
        small[128:136],
        small[136:144],
        g_rows[:, :16].reshape(128, width),
        small[64:128],
        wide(g_ff[:, :, :384]),
        wide(g_ff[:, :, 384:]),
        g_rows[:, 16:].reshape(192, width),
    )


def solution(mesh):
    fine = Mesh(mesh.devices.reshape(4, 4, 4, 2), ("y", "x", "z", "c"))
    every = ("y", "x", "z", "c")
    shard1 = P(SHARD)
    shard2 = P(SHARD, None)
    return jax.shard_map(
        local,
        mesh=fine,
        in_specs=(
            P(every, None), P(every), P(every, None), shard1, shard2, shard2, shard2,
            shard1, shard1, shard2, shard1, shard2, shard2, shard2,
        ),
        out_specs=(
            P(every, None), P(every, None), shard1, shard2, shard2, shard2,
            shard1, shard1, shard2, shard1, shard2, shard2, shard2,
        ),
        check_vma=False,
    )
```

```python
import math

import jax
import jax.numpy as jnp
from jax import lax
from jax.sharding import Mesh, PartitionSpec as P

EPSILON = 1e-06
THETA = 1000000.0
SHARD = ("y", "x")
NS = 16
BF = jnp.bfloat16
F32 = jnp.float32


def rms_forward(inputs, scales):
    factor = lax.rsqrt(jnp.mean(inputs * inputs, axis=-1, keepdims=True) + EPSILON)
    normed = inputs * factor
    return (normed * scales, normed, factor)


def rms_backward(grad_out, scales, normed, factor):
    grad_normed = grad_out * scales
    grad_in = factor * (
        grad_normed - normed * jnp.mean(grad_normed * normed, axis=-1, keepdims=True)
    )
    return (grad_in, jnp.sum(grad_out * normed, axis=tuple(range(grad_out.ndim - 1))))


def rope_tables(positions, head_dim):
    half_dim = head_dim // 2
    frequency = jnp.exp(
        jnp.arange(half_dim).astype(F32) * (-2.0 * math.log(THETA) / head_dim)
    )
    angles = positions.astype(F32)[..., None] * frequency
    return (jnp.cos(angles), jnp.sin(angles))


def rotate(inputs, cosine, sine):
    a, b = jnp.split(inputs, 2, axis=-1)
    return jnp.concatenate([a * cosine - b * sine, b * cosine + a * sine], axis=-1)


def inverse_rotation(grad_out, cosine, sine):
    a, b = jnp.split(grad_out, 2, axis=-1)
    return jnp.concatenate([a * cosine + b * sine, b * cosine - a * sine], axis=-1)


def mm(left, right):
    return jnp.dot(left, right, preferred_element_type=F32)


def mm_nt(left, right):
    return lax.dot_general(left, right, (((1,), (1,)), ((), ())), preferred_element_type=F32)


def mm_tn(left, right):
    return lax.dot_general(left, right, (((0,), (0,)), ((), ())), preferred_element_type=F32)


def spread(a):
    return lax.all_to_all(jnp.broadcast_to(a[None], (NS,) + a.shape), SHARD, 0, 0)


def scatter_shard(a):
    return lax.all_to_all(a.astype(BF), SHARD, 0, 0).astype(F32).sum(0)


def core_swap(a):
    return lax.ppermute(a, "c", [(0, 1), (1, 0)])


def near_swap(a):
    return lax.ppermute(a, "z", [(0, 1), (1, 0), (2, 3), (3, 2)])


def far_swap(a):
    return lax.ppermute(a, "z", [(0, 3), (3, 0), (1, 2), (2, 1)])


def gather_four(a):
    far = near_swap(a)
    return [a, core_swap(a), far, core_swap(far)]


def scatter_four(partial, rows):
    block = lambda k: partial[k * rows : (k + 1) * rows]
    got = core_swap(jnp.concatenate([block(1), block(3)], axis=0)).astype(F32)
    pair = block(2).astype(F32) + got[rows:]
    other = near_swap(pair.astype(BF))
    return block(0).astype(F32) + got[:rows] + other.astype(F32)


def after(a, *earlier):
    return lax.optimization_barrier((a,) + earlier)[0]


EVERY = ("y", "x", "z", "c")


def device(y, x, z, c):
    return ((y * 4 + x) * 4 + z) * 2 + c


def part_of(z, c):
    return (2 if z in (1, 2) else 0) + c


def own_heads(w_block):
    y, z, c = lax.axis_index("y"), lax.axis_index("z"), lax.axis_index("c")
    part = jnp.where((z == 1) | (z == 2), 2, 0) + c
    line = jnp.where(y == part, w_block, jnp.zeros_like(w_block))
    for k in (1, 2, 3):
        pairs = [
            (device(part_of(z, c), x, z, c), device((part_of(z, c) + k) % 4, x, z, c))
            for x in range(4)
            for z in range(4)
            for c in range(2)
        ]
        line = line + lax.ppermute(w_block, EVERY, pairs)
    x = lax.axis_index("x")
    near = [line] + [
        lax.ppermute(line, "x", [(i, (i + k) % 4) for i in range(4)]) for k in (1, 2, 3)
    ]
    near = jnp.stack(near, axis=0)
    return jnp.concatenate(
        [lax.dynamic_index_in_dim(near, (x - h) % 4, 0, False) for h in range(4)], axis=0
    )


def local(
    tokens,
    positions,
    cotangent,
    attn_gain,
    w_query,
    key_projection,
    value_projection,
    q_gain,
    k_gain,
    w_output,
    ffn_gain,
    w_gate,
    w_up,
    w_down,
):
    z, core = lax.axis_index("z"), lax.axis_index("c")
    part = jnp.where((z == 1) | (z == 2), 2, 0) + core
    rows = tokens.shape[0]
    width = tokens.shape[1]
    head = 128
    tall = 4 * rows
    cut = lambda w, n: lax.dynamic_slice_in_dim(w, part * n, n, 1)
    cut_rows = lambda w, n: lax.dynamic_slice_in_dim(w, part * n, n, 0)

    gains = jnp.concatenate([attn_gain, ffn_gain, q_gain, k_gain, jnp.zeros((880,), BF)])
    w_in = jnp.concatenate(
        [cut(w_query, 512), cut(key_projection, 256), cut(value_projection, 256)], axis=1
    )
    w_in = jnp.concatenate([w_in, gains[None], jnp.zeros((7, width), BF)], axis=0)
    w_in = spread(w_in)
    norm_one = w_in[:, 64, :64].reshape(-1).astype(F32)
    norm_two = w_in[:, 64, 64:128].reshape(-1).astype(F32)
    q_scale = w_in[:, 64, 128:136].reshape(-1).astype(F32)
    k_scale = w_in[:, 64, 136:144].reshape(-1).astype(F32)
    w_in = w_in[:, :64].reshape(width, 1024)

    x0 = jnp.concatenate(gather_four(tokens), axis=0)
    pos = jnp.stack(gather_four(positions), axis=0)
    cot = jnp.concatenate(gather_four(cotangent), axis=0)

    source = lax.broadcasted_iota(jnp.int32, (1536, 384), 0)
    target = lax.broadcasted_iota(jnp.int32, (1536, 384), 1)
    chosen = (source == 192 * (target // 48) + 48 * part + target % 48).astype(BF)
    pick = lambda w: jnp.concatenate(
        [mm(w[:, :1536], chosen).astype(BF), mm(w[:, 1536:], chosen).astype(BF)], axis=1
    )
    gate_cut, up_cut = pick(w_gate), pick(w_up)
    low = up_cut[:, 256:]
    w_ff = jnp.concatenate(
        [
            jnp.concatenate([gate_cut, up_cut[:, :256]], axis=1),
            jnp.concatenate([low[:32], low[32:]], axis=1),
            cut_rows(w_down, 48),
        ],
        axis=0,
    )
    w_ff = lax.all_gather(w_ff, SHARD, axis=0)
    w_dn = w_ff[:, 96:].reshape(768, width)
    low = jnp.concatenate([w_ff[:, 64:96, :512], w_ff[:, 64:96, 512:]], axis=1)
    w_ff = jnp.concatenate(
        [w_ff[:, :64].reshape(width, 1024), low.reshape(width, 512)], axis=1
    )

    w_out = own_heads(w_output)

    cosine, sine = rope_tables(pos, head)
    cosine, sine = cosine[:, :, None], sine[:, :, None]
    stream_in = tokens.astype(F32)
    first_out, first_unit, first_factor = rms_forward(x0.astype(F32), norm_one)
    first_unit, first_factor = first_unit[:rows], first_factor[:rows]
    x1 = first_out.astype(BF)

    raw = mm(x1, w_in)
    q_raw = raw[:, :512].reshape(4, rows, 4, head)
    k_raw = raw[:, 512:768].reshape(4, rows, 2, head)
    value = raw[:, 768:].astype(BF).reshape(4, rows, 2, head)
    q_normed, q_unit, q_factor = rms_forward(q_raw, q_scale)
    k_normed, k_unit, k_factor = rms_forward(k_raw, k_scale)
    query = rotate(q_normed, cosine, sine).astype(BF).reshape(4, rows, 2, 2, head)
    key = rotate(k_normed, cosine, sine).astype(BF)

    index = jnp.arange(rows, dtype=jnp.int32)
    starts = index[None, :] - pos
    mask = (index[None, None, :] <= index[None, :, None]) & (
        index[None, None, :] >= starts[:, :, None]
    )
    scores = jnp.einsum("bqjgd,bkjd->bjgqk", query, key, preferred_element_type=F32)
    scores = jnp.where(mask[:, None, None], scores * head ** (-0.5), -1e30)
    peak = jnp.max(scores, axis=-1, keepdims=True)
    weights = jnp.exp(scores - peak)
    probability = weights / jnp.sum(weights, axis=-1, keepdims=True)
    prob_low = probability.astype(BF)
    attended = jnp.einsum("bjgqk,bkjd->bqjgd", prob_low, value, preferred_element_type=F32)
    attended = attended.astype(BF)
    att = attended.reshape(tall, 512)

    middle = stream_in + scatter_four(mm(att, w_out).astype(BF), rows)
    second_out, second_unit, second_factor = rms_forward(middle, norm_two)
    x2 = jnp.concatenate(gather_four(second_out.astype(BF)), axis=0)

    both = mm(x2, w_ff)
    gate, upper = both[:, :768], both[:, 768:]
    sig = jax.nn.sigmoid(gate)
    hidden = (gate * sig * upper).astype(BF)

    grad_hidden = mm_nt(cot, w_dn)
    grad_gate_low = (grad_hidden * upper * sig * (1.0 + gate * (1.0 - sig))).astype(BF)
    grad_upper_low = (grad_hidden * gate * sig).astype(BF)
    grad_both = jnp.concatenate([grad_gate_low, grad_upper_low], axis=1)
    grad_second = scatter_four(mm_nt(grad_both, w_ff).astype(BF), rows)
    mixed = (middle + scatter_four(mm(hidden, w_dn).astype(BF), rows)).astype(BF)
    g_ff = mm_tn(x2, grad_both).astype(BF).reshape(NS, 64, 1536)
    g_dn = mm_tn(hidden, cot).astype(BF).reshape(NS, 48, width)
    low = g_ff[:, :, 1024:]
    g_ff = jnp.concatenate(
        [g_ff[:, :, :1024], jnp.concatenate([low[:, :32], low[:, 32:]], axis=2), g_dn], axis=1
    )
    grad_part, g_norm_two = rms_backward(grad_second, norm_two, second_unit, second_factor)
    grad_middle = cotangent.astype(F32) + grad_part
    gm = jnp.concatenate(gather_four(grad_middle.astype(BF)), axis=0)

    grad_att = mm_nt(gm, w_out).astype(BF).reshape(4, rows, 2, 2, head)
    g_out = mm_tn(att, gm).astype(BF)
    grad_value = jnp.einsum("bjgqk,bqjgd->bkjd", prob_low, grad_att, preferred_element_type=F32)
    grad_probs = jnp.einsum("bqjgd,bkjd->bjgqk", grad_att, value, preferred_element_type=F32)
    delta = jnp.sum(grad_att.astype(F32) * attended.astype(F32), axis=-1)
    grad_scores = (
        probability * (grad_probs - jnp.transpose(delta, (0, 2, 3, 1))[..., None]) * head ** (-0.5)
    ).astype(BF)
    grad_query = jnp.einsum("bjgqk,bkjd->bqjgd", grad_scores, key, preferred_element_type=F32)
    grad_key = jnp.einsum("bjgqk,bqjgd->bkjd", grad_scores, query, preferred_element_type=F32)
    grad_query, g_q = rms_backward(
        inverse_rotation(grad_query.reshape(4, rows, 4, head), cosine, sine),
        q_scale, q_unit, q_factor,
    )
    grad_key, g_k = rms_backward(
        inverse_rotation(grad_key, cosine, sine), k_scale, k_unit, k_factor
    )
    grad_in = jnp.concatenate(
        [
            grad_query.astype(BF).reshape(tall, 512),
            grad_key.astype(BF).reshape(tall, 256),
            grad_value.astype(BF).reshape(tall, 256),
        ],
        axis=1,
    )
    g_in = mm_tn(x1, grad_in).astype(BF).reshape(NS, 64, 1024)
    grad_first = scatter_four(mm_nt(grad_in, w_in).astype(BF), rows)
    grad_part, g_norm_one = rms_backward(grad_first, norm_one, first_unit, first_factor)
    grad_tokens = (grad_middle + grad_part).astype(BF)

    def finish(g):
        g = (g + far_swap(g.astype(BF)).astype(F32)).astype(BF)
        whole = jnp.stack(gather_four(g), axis=0)
        return [lax.dynamic_index_in_dim(whole, k ^ part, 0, False) for k in range(4)]

    g_ff = lax.psum_scatter(g_ff, SHARD, scatter_dimension=0)
    g_ff = finish(g_ff.astype(F32))
    g_out = jnp.transpose(g_out.reshape(4, NS, 8, width), (1, 0, 2, 3)).reshape(NS, 32, width)
    g_out = scatter_shard(g_out)
    g_in = scatter_shard(after(g_in, g_out))
    g_out = finish(g_out)
    g_in_sum = g_in
    g_in = finish(g_in)
    g_out = jnp.concatenate([g.reshape(4, 8, width) for g in g_out], axis=0)
    small = jnp.concatenate(
        [
            g_norm_one.reshape(NS, 64),
            g_norm_two.reshape(NS, 64),
            g_q.reshape(NS, 8),
            g_k.reshape(NS, 8),
            jnp.zeros((NS, width - 144), F32),
        ],
        axis=1,
    ).astype(BF)
    last = jnp.concatenate([g_out, small[:, None], jnp.zeros((NS, 7, width), BF)], axis=1)
    last = lax.all_to_all(after(last, g_in_sum), SHARD, 0, 0)
    g_out = last[:, :8].reshape(128, width).astype(F32)
    small = last[:, 8, :256].astype(F32).sum(0).reshape(2, 128)
    small = small + far_swap(small)
    small = small + near_swap(small)
    small = (small + core_swap(small)).reshape(256)

    def hidden_order(pieces):
        source = lax.broadcasted_iota(jnp.int32, (1536, 1536), 0)
        target = lax.broadcasted_iota(jnp.int32, (1536, 1536), 1)
        at, k = target // 192, target % 192
        order = (source == 384 * (k // 48) + 48 * at + k % 48).astype(BF)
        half = lambda j: mm(
            jnp.concatenate([p[:, 384 * j : 384 * j + 384] for p in pieces], axis=1), order
        )
        return jnp.concatenate([half(0), half(1)], axis=1)

    lows = [jnp.concatenate([g[64:96, :512], g[64:96, 512:]], axis=0) for g in g_ff]
    pieces = [
        jnp.concatenate([g[:64, :768], jnp.concatenate([g[:64, 768:], l], axis=1)], axis=0)
        for g, l in zip(g_ff, lows)
    ]
    g_gu = hidden_order(pieces)
    side = lambda a, b: jnp.concatenate([g[:, a:b].astype(F32) for g in g_in], axis=1)
    return (
        mixed,
        grad_tokens,
        small[:64],
        side(0, 512),
        side(512, 768),
        side(768, 1024),
        small[128:136],
        small[136:144],
        g_out,
        small[64:128],
        g_gu[:64],
        g_gu[64:],
        jnp.concatenate([g[96:].astype(F32) for g in g_ff], axis=0),
    )


def solution(mesh):
    fine = Mesh(mesh.devices.reshape(4, 4, 4, 2), ("y", "x", "z", "c"))
    every = ("y", "x", "z", "c")
    shard1 = P(SHARD)
    shard2 = P(SHARD, None)
    return jax.shard_map(
        local,
        mesh=fine,
        in_specs=(
            P(every, None), P(every), P(every, None), shard1, shard2, shard2, shard2,
            shard1, shard1, shard2, shard1, shard2, shard2, shard2,
        ),
        out_specs=(
            P(every, None), P(every, None), shard1, shard2, shard2, shard2,
            shard1, shard1, shard2, shard1, shard2, shard2, shard2,
        ),
        check_vma=False,
    )
```

```python
import math

import jax
import jax.numpy as jnp
from jax import lax
from jax.experimental import pallas as pl
from jax.experimental.pallas import tpu as pltpu
from jax.sharding import Mesh, PartitionSpec as P

EPSILON = 1e-06
THETA = 1000000.0
SHARD = ("y", "x")
NS = 16
BF = jnp.bfloat16
F32 = jnp.float32


def rms_forward(inputs, scales):
    factor = lax.rsqrt(jnp.mean(inputs * inputs, axis=-1, keepdims=True) + EPSILON)
    normed = inputs * factor
    return (normed * scales, normed, factor)


def rms_backward(grad_out, scales, normed, factor):
    grad_normed = grad_out * scales
    return factor * (
        grad_normed - normed * jnp.mean(grad_normed * normed, axis=-1, keepdims=True)
    )


def rope_tables(positions, head_dim):
    half_dim = head_dim // 2
    frequency = jnp.exp(
        jnp.arange(half_dim).astype(F32) * (-2.0 * math.log(THETA) / head_dim)
    )
    angles = positions.astype(F32)[..., None] * frequency
    return (jnp.cos(angles), jnp.sin(angles))


def mm(left, right):
    return jnp.dot(left, right, preferred_element_type=F32)


def mm_nt(left, right):
    return lax.dot_general(left, right, (((1,), (1,)), ((), ())), preferred_element_type=F32)


def mm_tn(left, right):
    return lax.dot_general(left, right, (((0,), (0,)), ((), ())), preferred_element_type=F32)


def whole(shape, dtype):
    return jax.ShapeDtypeStruct(shape, dtype)


def turned(a, cosine, sine):
    return a * cosine + pltpu.roll(a, 64, axis=1) * sine


def attention_forward(
    w_all, x0, cosine, sine, position,
    x1, raw, query, key, value, prob, att, w_in, gains,
):
    rows = 144
    w_in[...] = w_all[:, :64, :].reshape(1024, 1024)
    gains[...] = w_all[:, 64:, :].astype(F32).sum(0)
    norm_one = gains[0:1, :]
    q_scale, k_scale = gains[2:3, :128], gains[2:3, 128:256]
    stream = x0[...].astype(F32)
    factor = lax.rsqrt(jnp.mean(stream * stream, axis=-1, keepdims=True) + EPSILON)
    x1[...] = (stream * factor * norm_one).astype(BF)
    cos, sin = cosine[...], sine[...]
    for h in range(8):
        at = slice(128 * h, 128 * h + 128)
        if h % 2 == 0:
            two = mm(x1[...], w_in[:, 128 * h : 128 * h + 256])
        part = two[:, 128 * (h % 2) : 128 * (h % 2) + 128]
        if h < 6:
            raw[:, at] = part
            scale = q_scale if h < 4 else k_scale
            factor = lax.rsqrt(jnp.mean(part * part, axis=-1, keepdims=True) + EPSILON)
            done = turned(part * factor * scale, cos, sin).astype(BF)
            if h < 4:
                query[:, at] = done
            else:
                key[:, 128 * (h - 4) : 128 * (h - 4) + 128] = done
        else:
            value[:, 128 * (h - 6) : 128 * (h - 6) + 128] = part.astype(BF)
    near = lax.broadcasted_iota(jnp.int32, (rows, rows), 1)
    this = lax.broadcasted_iota(jnp.int32, (rows, rows), 0)
    for b in range(4):
        own = slice(rows * b, rows * b + rows)
        allowed = (near <= this) & (near >= this - position[own, :])
        allowed = jnp.concatenate([allowed.astype(F32)] * 2, axis=0) > 0.5
        for j in range(2):
            kv = slice(128 * j, 128 * j + 128)
            one = slice(256 * j, 256 * j + 128)
            two = slice(256 * j + 128, 256 * j + 256)
            q = jnp.concatenate([query[own, one], query[own, two]], axis=0)
            scores = jnp.where(allowed, mm_nt(q, key[own, kv]) * 128 ** (-0.5), -1e30)
            weights = jnp.exp(scores - jnp.max(scores, axis=-1, keepdims=True))
            p = weights / jnp.sum(weights, axis=-1, keepdims=True)
            prob[2 * b + j] = p
            out = mm(p.astype(BF), value[own, kv]).astype(BF)
            att[own, one] = out[:rows]
            att[own, two] = out[rows:]


def attention_backward(
    gm, w_out, att, raw, query, key, value, prob, q_scale, k_scale, cosine, sine,
    grad_in, g_q, g_k, grad_att, d_query, d_key,
):
    rows = 144
    grad_att[...] = mm_nt(gm[...], w_out[...]).astype(BF)
    for b in range(4):
        own = slice(rows * b, rows * b + rows)
        for j in range(2):
            kv = slice(128 * j, 128 * j + 128)
            one = slice(256 * j, 256 * j + 128)
            two = slice(256 * j + 128, 256 * j + 256)
            both = lambda ref: jnp.concatenate([ref[own, one], ref[own, two]], axis=0)
            p = prob[2 * b + j]
            d_out = both(grad_att)
            grad_in[own, 768 + 128 * j : 896 + 128 * j] = mm_tn(p.astype(BF), d_out).astype(BF)
            d_prob = mm_nt(d_out, value[own, kv])
            delta = jnp.sum(
                d_out.astype(F32) * both(att).astype(F32), axis=-1, keepdims=True
            )
            d_scores = (p * (d_prob - delta) * 128 ** (-0.5)).astype(BF)
            d_q = mm(d_scores, key[own, kv])
            d_query[own, one] = d_q[:rows]
            d_query[own, two] = d_q[rows:]
            d_key[own, kv] = mm_tn(d_scores, both(query))
    cos, sin = cosine[...], sine[...]
    for h in range(6):
        at = slice(128 * h, 128 * h + 128)
        part = raw[:, at]
        factor = lax.rsqrt(jnp.mean(part * part, axis=-1, keepdims=True) + EPSILON)
        unit = part * factor
        if h < 4:
            e, scale, total_ref = d_query[:, at], q_scale[...], g_q
        else:
            e, scale, total_ref = d_key[:, 128 * (h - 4) : 128 * (h - 4) + 128], k_scale[...], g_k
        e = turned(e, cos, -sin)
        line = jnp.sum(e * unit, axis=0, keepdims=True)
        total_ref[...] = line if h in (0, 4) else total_ref[...] + line
        e = e * scale
        grad_in[:, at] = (
            factor * (e - unit * jnp.mean(e * unit, axis=-1, keepdims=True))
        ).astype(BF)


def run_forward(w_all, x0, cosine, sine, position):
    tall = x0.shape[0]
    return pl.pallas_call(
        attention_forward,
        out_shape=(
            whole((tall, 1024), BF),
            whole((tall, 768), F32),
            whole((tall, 512), BF),
            whole((tall, 256), BF),
            whole((tall, 256), BF),
            whole((8, 288, 144), F32),
            whole((tall, 512), BF),
            whole((1024, 1024), BF),
            whole((16, 1024), F32),
        ),
        compiler_params=pltpu.CompilerParams(vmem_limit_bytes=56 << 20),
        cost_estimate=pl.CostEstimate(
            flops=1_600_000_000, transcendentals=400_000, bytes_accessed=12_000_000
        ),
        name="attention_forward",
    )(w_all, x0, cosine, sine, position)


def run_backward(gm, w_out, att, raw, query, key, value, prob, q_scale, k_scale, cosine, sine):
    tall = gm.shape[0]
    return pl.pallas_call(
        attention_backward,
        out_shape=(
            whole((tall, 1024), BF),
            whole((1, 128), F32),
            whole((1, 128), F32),
        ),
        scratch_shapes=[
            pltpu.VMEM((tall, 512), BF),
            pltpu.VMEM((tall, 512), F32),
            pltpu.VMEM((tall, 256), F32),
        ],
        compiler_params=pltpu.CompilerParams(vmem_limit_bytes=56 << 20),
        cost_estimate=pl.CostEstimate(
            flops=1_200_000_000, transcendentals=4_000, bytes_accessed=12_000_000
        ),
        name="attention_backward",
    )(gm, w_out, att, raw, query, key, value, prob, q_scale, k_scale, cosine, sine)


def feed_forward(
    a0, a1, a2, a3, t0, t1, t2, t3, w_gu,
    x2, cot, hidden, grads, keep, send, w_dn, w_low, up_low, both, grad_hidden,
):
    rows = 144
    for k, (a, t) in enumerate(((a0, t0), (a1, t1), (a2, t2), (a3, t3))):
        x2[rows * k : rows * k + rows, :] = a[...]
        cot[rows * k : rows * k + rows, :] = t[rows:, :]
    w_high = w_gu[:, :64, :].reshape(1024, 1024)
    w_low[...] = jnp.concatenate(
        [w_gu[:, 64:96, :512], w_gu[:, 64:96, 512:]], axis=1
    ).reshape(1024, 512)
    both[...] = mm(x2[...], w_high)
    up_low[...] = mm(x2[...], w_low[...])
    w_dn[...] = w_gu[:, 96:, :].reshape(768, 1024)
    grad_hidden[...] = mm_nt(cot[...], w_dn[...])
    for k in range(6):
        at = slice(128 * k, 128 * k + 128)
        gate = both[:, at]
        up = both[:, 768 + 128 * k : 896 + 128 * k] if k < 2 else up_low[:, 128 * k - 256 : 128 * k - 128]
        e = grad_hidden[:, at]
        sig = jax.nn.sigmoid(gate)
        hidden[:, at] = (gate * sig * up).astype(BF)
        grads[:, at] = (e * up * sig * (1.0 + gate * (1.0 - sig))).astype(BF)
        grads[:, 768 + 128 * k : 896 + 128 * k] = (e * gate * sig).astype(BF)
    partial = mm_nt(grads[:, :1024], w_high) + mm_nt(grads[:, 1024:], w_low[...])
    partial = partial.astype(BF)
    keep[:rows, :] = partial[:rows]
    send[:rows, :] = partial[rows : 2 * rows]
    keep[rows:, :] = partial[2 * rows : 3 * rows]
    send[rows:, :] = partial[3 * rows :]


def feed_forward_weights(x2, high, low, hidden, cot, out):
    g = mm_tn(x2[...], high[...]).astype(BF)
    out[:, :64, :] = g.reshape(NS, 64, 256)
    g = mm_tn(x2[...], low[...]).astype(BF).reshape(NS, 64, 128)
    out[:, 64:96, :128] = g[:, :32]
    out[:, 64:96, 128:] = g[:, 32:]
    g = mm_tn(hidden[...], cot[...]).astype(BF)
    out[:, 96:, :] = g.reshape(NS, 48, 256)


def run_feed_forward(a, t, w_gu):
    tall, half = 576, 288
    return pl.pallas_call(
        feed_forward,
        out_shape=(
            whole((tall, 1024), BF),
            whole((tall, 1024), BF),
            whole((tall, 768), BF),
            whole((tall, 1536), BF),
            whole((half, 1024), BF),
            whole((half, 1024), BF),
            whole((768, 1024), BF),
        ),
        scratch_shapes=[
            pltpu.VMEM((1024, 512), BF),
            pltpu.VMEM((tall, 512), F32),
            pltpu.VMEM((tall, 1024), F32),
            pltpu.VMEM((tall, 768), F32),
        ],
        compiler_params=pltpu.CompilerParams(vmem_limit_bytes=56 << 20),
        cost_estimate=pl.CostEstimate(
            flops=4_600_000_000, transcendentals=450_000, bytes_accessed=16_000_000
        ),
        name="feed_forward",
    )(*a, *t, w_gu)


def run_feed_forward_weights(x2, grads, hidden, cot):
    tall = x2.shape[0]
    return pl.pallas_call(
        feed_forward_weights,
        grid=(4,),
        in_specs=[
            pl.BlockSpec((tall, 1024), lambda k: (0, 0)),
            pl.BlockSpec((tall, 256), lambda k: (0, k)),
            pl.BlockSpec((tall, 128), lambda k: (0, 8 + k)),
            pl.BlockSpec((tall, 768), lambda k: (0, 0)),
            pl.BlockSpec((tall, 256), lambda k: (0, k)),
        ],
        out_specs=pl.BlockSpec((NS, 144, 256), lambda k: (0, 0, k)),
        out_shape=whole((NS, 144, 1024), BF),
        compiler_params=pltpu.CompilerParams(vmem_limit_bytes=56 << 20),
        cost_estimate=pl.CostEstimate(
            flops=2_700_000_000, transcendentals=0, bytes_accessed=10_000_000
        ),
        name="feed_forward_weights",
    )(x2, grads, grads, hidden, cot)


def scatter_shard(a):
    return lax.all_to_all(a, SHARD, 0, 0).astype(F32).sum(0)


def core_swap(a):
    return lax.ppermute(a, "c", [(0, 1), (1, 0)])


def near_swap(a):
    return lax.ppermute(a, "z", [(0, 1), (1, 0), (2, 3), (3, 2)])


def far_swap(a):
    return lax.ppermute(a, "z", [(0, 3), (3, 0), (1, 2), (2, 1)])


def gather_four(a):
    far = near_swap(a)
    return [a, core_swap(a), far, core_swap(far)]


def scatter_four(keep, send):
    rows = keep.shape[0] // 2
    got = core_swap(send).astype(F32)
    pair = keep[rows:].astype(F32) + got[rows:]
    other = near_swap(pair.astype(BF))
    return keep[:rows].astype(F32) + got[:rows] + other.astype(F32)


def halves(partial, rows):
    block = lambda k: partial[k * rows : (k + 1) * rows]
    return (
        jnp.concatenate([block(0), block(2)], axis=0),
        jnp.concatenate([block(1), block(3)], axis=0),
    )


def after(a, *earlier):
    return lax.optimization_barrier((a,) + earlier)[0]


EVERY = ("y", "x", "z", "c")


def device(y, x, z, c):
    return ((y * 4 + x) * 4 + z) * 2 + c


def part_of(z, c):
    return (2 if z in (1, 2) else 0) + c


def column_heads(w_block):
    y, z, c = lax.axis_index("y"), lax.axis_index("z"), lax.axis_index("c")
    part = jnp.where((z == 1) | (z == 2), 2, 0) + c
    line = jnp.where(y == part, w_block, jnp.zeros_like(w_block))
    for k in (1, 2, 3):
        pairs = [
            (device(part_of(z, c), x, z, c), device((part_of(z, c) + k) % 4, x, z, c))
            for x in range(4)
            for z in range(4)
            for c in range(2)
        ]
        line = line + lax.ppermute(w_block, EVERY, pairs)
    return line


def line_heads(line):
    x = lax.axis_index("x")
    near = [line] + [
        lax.ppermute(line, "x", [(i, (i + k) % 4) for i in range(4)]) for k in (1, 2, 3)
    ]
    near = jnp.stack(near, axis=0)
    return jnp.concatenate(
        [lax.dynamic_index_in_dim(near, (x - h) % 4, 0, False) for h in range(4)], axis=0
    )


def local(
    tokens,
    positions,
    cotangent,
    attn_gain,
    w_query,
    key_projection,
    value_projection,
    q_gain,
    k_gain,
    w_output,
    ffn_gain,
    w_gate,
    w_up,
    w_down,
):
    z, core = lax.axis_index("z"), lax.axis_index("c")
    part = jnp.where((z == 1) | (z == 2), 2, 0) + core
    rows = tokens.shape[0]
    width = tokens.shape[1]
    head = 128
    tall = 4 * rows
    cut = lambda w, n: lax.dynamic_slice_in_dim(w, part * n, n, 1)
    cut_rows = lambda w, n: lax.dynamic_slice_in_dim(w, part * n, n, 0)

    member = 4 * lax.axis_index("y") + lax.axis_index("x")
    lane = lax.broadcasted_iota(jnp.int32, (16, width), 1)
    row = lax.broadcasted_iota(jnp.int32, (16, width), 0)
    again = lambda g: jnp.tile(g, (width // g.shape[0],))[None]
    q_lane = (lane // 8) == member
    k_lane = (lane // 8) == member + 16
    gain_rows = jnp.where(
        row < 2,
        jnp.where((lane // 64) == member, jnp.where(row == 0, again(attn_gain), again(ffn_gain)), 0),
        jnp.where(q_lane, again(q_gain), jnp.where(k_lane, again(k_gain), 0)),
    ).astype(BF)
    w_in = jnp.concatenate(
        [cut(w_query, 512), cut(key_projection, 256), cut(value_projection, 256)], axis=1
    )
    w_in = jnp.concatenate([w_in, gain_rows], axis=0)

    w_in = lax.all_gather(w_in, SHARD, axis=0)
    w_out = line_heads(column_heads(w_output))

    own = gather_four(jnp.concatenate([tokens, cotangent], axis=0))
    pos = jnp.stack(gather_four(positions), axis=0)
    x0 = jnp.concatenate([a[:rows] for a in own], axis=0)
    w_in, w_out, x0, pos = lax.optimization_barrier((w_in, w_out, x0, pos))

    source = lax.broadcasted_iota(jnp.int32, (1536, 384), 0)
    target = lax.broadcasted_iota(jnp.int32, (1536, 384), 1)
    chosen = (source == 192 * (target // 48) + 48 * part + target % 48).astype(BF)
    pick = lambda w: jnp.concatenate(
        [mm(w[:, :1536], chosen).astype(BF), mm(w[:, 1536:], chosen).astype(BF)], axis=1
    )
    gate_cut, up_cut = pick(w_gate), pick(w_up)
    low = up_cut[:, 256:]
    w_ff = jnp.concatenate(
        [
            jnp.concatenate([gate_cut, up_cut[:, :256]], axis=1),
            jnp.concatenate([low[:32], low[32:]], axis=1),
            cut_rows(w_down, 48),
        ],
        axis=0,
    )
    w_ff = lax.all_gather(after(w_ff, w_in), SHARD, axis=0)


    cosine, sine = rope_tables(pos.reshape(-1), head)
    cosine = jnp.concatenate([cosine, cosine], axis=-1)
    sine = jnp.concatenate([-sine, sine], axis=-1)
    stream_in = tokens.astype(F32)
    x1, raw, query, key, value, prob, att, w_in, gains = run_forward(
        w_in, x0, cosine, sine, pos.reshape(-1, 1)
    )
    norm_one, norm_two = gains[0], gains[1]
    scales = (gains[2:3, :128], gains[2:3, 128:256], cosine, sine)

    middle = stream_in + scatter_four(*halves(mm(att, w_out).astype(BF), rows))
    second_out, second_unit, second_factor = rms_forward(middle, norm_two)
    x2, cot, hidden, grads, keep, send, w_dn = run_feed_forward(
        gather_four(second_out.astype(BF)), own, w_ff
    )
    g_ff = run_feed_forward_weights(x2, grads, hidden, cot)
    g_ff_sum = lax.psum_scatter(g_ff, SHARD, scatter_dimension=0)
    grad_second = after(scatter_four(keep, send), g_ff)
    grad_part = rms_backward(grad_second, norm_two, second_unit, second_factor)
    grad_middle = cotangent.astype(F32) + grad_part
    gm = jnp.concatenate(gather_four(grad_middle.astype(BF)), axis=0)
    mixed = scatter_four(*halves(after(mm(hidden, w_dn).astype(BF), gm), rows))
    mixed = (middle + mixed).astype(BF)

    g_out = mm_tn(att, gm).astype(BF).reshape(4, NS, 8, width)
    g_out = jnp.transpose(g_out, (1, 0, 2, 3)).reshape(NS, 32, width)
    g_out_sum = lax.all_to_all(g_out, SHARD, 0, 0)
    grad_in, g_q, g_k = run_backward(after(gm, g_out), w_out, att, raw, query, key, value, prob, *scales)
    g_in = mm_tn(x1, grad_in).astype(BF).reshape(NS, 64, 1024)
    grad_in = after(grad_in, g_in)
    grad_first = scatter_four(*halves(mm_nt(grad_in, w_in).astype(BF), rows))
    _, first_unit, first_factor = rms_forward(stream_in, norm_one)
    grad_part = rms_backward(grad_first, norm_one, first_unit, first_factor)
    grad_tokens = (grad_middle + grad_part).astype(BF)

    def finish(g):
        whole_g = jnp.stack(gather_four(g), axis=0)
        return [lax.dynamic_index_in_dim(whole_g, k ^ part, 0, False) for k in range(4)]

    pair = lambda g: (g + far_swap(g.astype(BF)).astype(F32)).astype(BF)
    g_out = finish(pair(g_out_sum.astype(F32).sum(0)))
    g_out = jnp.concatenate([g.reshape(4, 8, width) for g in g_out], axis=0)
    heads = jnp.concatenate(
        [g_q.reshape(NS, 1, 8), g_k.reshape(NS, 1, 8), jnp.zeros((NS, 1, width - 16), F32)], axis=2
    ).astype(BF)
    last = jnp.concatenate([g_in, heads, jnp.zeros((NS, 7, width), BF), g_out], axis=1)
    last = lax.all_to_all(last, SHARD, 0, 0)
    g_in = finish(pair(last[:, :72].astype(F32).sum(0)))
    g_ff = finish(pair(g_ff_sum.astype(F32)))
    g_out = last[:, 72:].reshape(128, width).astype(F32)
    heads = sum(g[64, :16].astype(F32) for g in g_in)
    side = lambda a, b: jnp.concatenate([g[:64, a:b].astype(F32) for g in g_in], axis=1)
    g_q, g_k, g_v = side(0, 512), side(512, 768), side(768, 1024)

    def hidden_order(pieces):
        source = lax.broadcasted_iota(jnp.int32, (1536, 1536), 0)
        target = lax.broadcasted_iota(jnp.int32, (1536, 1536), 1)
        at, k = target // 192, target % 192
        order = (source == 384 * (k // 48) + 48 * at + k % 48).astype(BF)
        half = lambda j: mm(
            jnp.concatenate([p[:, 384 * j : 384 * j + 384] for p in pieces], axis=1), order
        )
        return jnp.concatenate([half(0), half(1)], axis=1)

    halved = lambda g, k: jnp.concatenate(
        [g[64:96, 256 * k : 256 * k + 128], g[64:96, 256 * k + 128 : 256 * k + 256]], axis=0
    )
    lows = [jnp.concatenate([halved(g, k) for k in range(4)], axis=1) for g in g_ff]
    pieces = [
        jnp.concatenate([g[:64, :768], jnp.concatenate([g[:64, 768:], l], axis=1)], axis=0)
        for g, l in zip(g_ff, lows)
    ]
    g_gu = hidden_order(pieces)
    row = lambda w, g: jnp.sum(w.astype(F32) * g, axis=1)
    g_norm_one = row(w_query, g_q) + row(key_projection, g_k) + row(value_projection, g_v)
    g_norm_two = row(w_gate, g_gu[:64]) + row(w_up, g_gu[64:])
    return (
        mixed,
        grad_tokens,
        g_norm_one / attn_gain.astype(F32),
        g_q,
        g_k,
        g_v,
        heads[:8],
        heads[8:],
        g_out,
        g_norm_two / ffn_gain.astype(F32),
        g_gu[:64],
        g_gu[64:],
        jnp.concatenate([g[96:].astype(F32) for g in g_ff], axis=0),
    )


def solution(mesh):
    fine = Mesh(mesh.devices.reshape(4, 4, 4, 2), ("y", "x", "z", "c"))
    every = ("y", "x", "z", "c")
    shard1 = P(SHARD)
    shard2 = P(SHARD, None)
    return jax.shard_map(
        local,
        mesh=fine,
        in_specs=(
            P(every, None), P(every), P(every, None), shard1, shard2, shard2, shard2,
            shard1, shard1, shard2, shard1, shard2, shard2, shard2,
        ),
        out_specs=(
            P(every, None), P(every, None), shard1, shard2, shard2, shard2,
            shard1, shard1, shard2, shard1, shard2, shard2, shard2,
        ),
        check_vma=False,
    )
```

```python
import math

import jax
import jax.numpy as jnp
from jax import lax
from jax.experimental import pallas as pl
from jax.experimental.pallas import tpu as pltpu
from jax.sharding import Mesh, PartitionSpec as P

EPSILON = 1e-06
THETA = 1000000.0
SHARD = ("y", "x")
NS = 16
BF = jnp.bfloat16
F32 = jnp.float32


def rms_forward(inputs, scales):
    factor = lax.rsqrt(jnp.mean(inputs * inputs, axis=-1, keepdims=True) + EPSILON)
    normed = inputs * factor
    return (normed * scales, normed, factor)


def rms_backward(grad_out, scales, normed, factor):
    grad_normed = grad_out * scales
    return factor * (
        grad_normed - normed * jnp.mean(grad_normed * normed, axis=-1, keepdims=True)
    )


def rope_tables(positions, head_dim):
    half_dim = head_dim // 2
    frequency = jnp.exp(
        jnp.arange(half_dim).astype(F32) * (-2.0 * math.log(THETA) / head_dim)
    )
    angles = positions.astype(F32)[..., None] * frequency
    return (jnp.cos(angles), jnp.sin(angles))


def mm(left, right):
    return jnp.dot(left, right, preferred_element_type=F32)


def mm_nt(left, right):
    return lax.dot_general(left, right, (((1,), (1,)), ((), ())), preferred_element_type=F32)


def mm_tn(left, right):
    return lax.dot_general(left, right, (((0,), (0,)), ((), ())), preferred_element_type=F32)


def whole(shape, dtype):
    return jax.ShapeDtypeStruct(shape, dtype)


def turned(a, cosine, sine):
    return a * cosine + pltpu.roll(a, 64, axis=1) * sine


def attention_forward(
    w_all, x0, cosine, sine, position,
    x1, raw, query, key, value, prob, att, w_in, gains,
):
    rows = 144
    w_in[...] = w_all[:, :64, :].reshape(1024, 1024)
    gains[...] = w_all[:, 64:, :].astype(F32).sum(0)
    norm_one = gains[0:1, :]
    q_scale, k_scale = gains[2:3, :128], gains[2:3, 128:256]
    stream = x0[...].astype(F32)
    factor = lax.rsqrt(jnp.mean(stream * stream, axis=-1, keepdims=True) + EPSILON)
    x1[...] = (stream * factor * norm_one).astype(BF)
    cos, sin = cosine[...], sine[...]
    for h in range(8):
        at = slice(128 * h, 128 * h + 128)
        if h % 2 == 0:
            two = mm(x1[...], w_in[:, 128 * h : 128 * h + 256])
        part = two[:, 128 * (h % 2) : 128 * (h % 2) + 128]
        if h < 6:
            raw[:, at] = part
            scale = q_scale if h < 4 else k_scale
            factor = lax.rsqrt(jnp.mean(part * part, axis=-1, keepdims=True) + EPSILON)
            done = turned(part * factor * scale, cos, sin).astype(BF)
            if h < 4:
                query[:, at] = done
            else:
                key[:, 128 * (h - 4) : 128 * (h - 4) + 128] = done
        else:
            value[:, 128 * (h - 6) : 128 * (h - 6) + 128] = part.astype(BF)
    near = lax.broadcasted_iota(jnp.int32, (rows, rows), 1)
    this = lax.broadcasted_iota(jnp.int32, (rows, rows), 0)
    for b in range(4):
        own = slice(rows * b, rows * b + rows)
        allowed = (near <= this) & (near >= this - position[own, :])
        allowed = jnp.concatenate([allowed.astype(F32)] * 2, axis=0) > 0.5
        for j in range(2):
            kv = slice(128 * j, 128 * j + 128)
            one = slice(256 * j, 256 * j + 128)
            two = slice(256 * j + 128, 256 * j + 256)
            q = jnp.concatenate([query[own, one], query[own, two]], axis=0)
            scores = jnp.where(allowed, mm_nt(q, key[own, kv]) * 128 ** (-0.5), -1e30)
            weights = jnp.exp(scores - jnp.max(scores, axis=-1, keepdims=True))
            p = weights / jnp.sum(weights, axis=-1, keepdims=True)
            prob[2 * b + j] = p
            out = mm(p.astype(BF), value[own, kv]).astype(BF)
            att[own, one] = out[:rows]
            att[own, two] = out[rows:]


def attention_backward(
    gm, w_out, att, raw, query, key, value, prob, q_scale, k_scale, cosine, sine,
    grad_in, g_q, g_k, grad_att, d_query, d_key,
):
    rows = 144
    grad_att[...] = mm_nt(gm[...], w_out[...]).astype(BF)
    for b in range(4):
        own = slice(rows * b, rows * b + rows)
        for j in range(2):
            kv = slice(128 * j, 128 * j + 128)
            one = slice(256 * j, 256 * j + 128)
            two = slice(256 * j + 128, 256 * j + 256)
            both = lambda ref: jnp.concatenate([ref[own, one], ref[own, two]], axis=0)
            p = prob[2 * b + j]
            d_out = both(grad_att)
            grad_in[own, 768 + 128 * j : 896 + 128 * j] = mm_tn(p.astype(BF), d_out).astype(BF)
            d_prob = mm_nt(d_out, value[own, kv])
            delta = jnp.sum(
                d_out.astype(F32) * both(att).astype(F32), axis=-1, keepdims=True
            )
            d_scores = (p * (d_prob - delta) * 128 ** (-0.5)).astype(BF)
            d_q = mm(d_scores, key[own, kv])
            d_query[own, one] = d_q[:rows]
            d_query[own, two] = d_q[rows:]
            d_key[own, kv] = mm_tn(d_scores, both(query))
    cos, sin = cosine[...], sine[...]
    for h in range(6):
        at = slice(128 * h, 128 * h + 128)
        part = raw[:, at]
        factor = lax.rsqrt(jnp.mean(part * part, axis=-1, keepdims=True) + EPSILON)
        unit = part * factor
        if h < 4:
            e, scale, total_ref = d_query[:, at], q_scale[...], g_q
        else:
            e, scale, total_ref = d_key[:, 128 * (h - 4) : 128 * (h - 4) + 128], k_scale[...], g_k
        e = turned(e, cos, -sin)
        line = jnp.sum(e * unit, axis=0, keepdims=True)
        total_ref[...] = line if h in (0, 4) else total_ref[...] + line
        e = e * scale
        grad_in[:, at] = (
            factor * (e - unit * jnp.mean(e * unit, axis=-1, keepdims=True))
        ).astype(BF)


def run_forward(w_all, x0, cosine, sine, position):
    tall = x0.shape[0]
    return pl.pallas_call(
        attention_forward,
        out_shape=(
            whole((tall, 1024), BF),
            whole((tall, 768), F32),
            whole((tall, 512), BF),
            whole((tall, 256), BF),
            whole((tall, 256), BF),
            whole((8, 288, 144), F32),
            whole((tall, 512), BF),
            whole((1024, 1024), BF),
            whole((16, 1024), F32),
        ),
        compiler_params=pltpu.CompilerParams(vmem_limit_bytes=56 << 20),
        cost_estimate=pl.CostEstimate(
            flops=1_600_000_000, transcendentals=400_000, bytes_accessed=12_000_000
        ),
        name="attention_forward",
    )(w_all, x0, cosine, sine, position)


def run_backward(gm, w_out, att, raw, query, key, value, prob, q_scale, k_scale, cosine, sine):
    tall = gm.shape[0]
    return pl.pallas_call(
        attention_backward,
        out_shape=(
            whole((tall, 1024), BF),
            whole((1, 128), F32),
            whole((1, 128), F32),
        ),
        scratch_shapes=[
            pltpu.VMEM((tall, 512), BF),
            pltpu.VMEM((tall, 512), F32),
            pltpu.VMEM((tall, 256), F32),
        ],
        compiler_params=pltpu.CompilerParams(vmem_limit_bytes=56 << 20),
        cost_estimate=pl.CostEstimate(
            flops=1_200_000_000, transcendentals=4_000, bytes_accessed=12_000_000
        ),
        name="attention_backward",
    )(gm, w_out, att, raw, query, key, value, prob, q_scale, k_scale, cosine, sine)


def feed_forward(
    a0, a1, a2, a3, t0, t1, t2, t3, w_gu,
    x2, cot, hidden, grads, keep, send, w_dn, w_low, up_low, both, grad_hidden,
):
    rows = 144
    for k, (a, t) in enumerate(((a0, t0), (a1, t1), (a2, t2), (a3, t3))):
        x2[rows * k : rows * k + rows, :] = a[...]
        cot[rows * k : rows * k + rows, :] = t[rows:, :]
    w_high = w_gu[:, :64, :].reshape(1024, 1024)
    w_low[...] = jnp.concatenate(
        [w_gu[:, 64:96, :512], w_gu[:, 64:96, 512:]], axis=1
    ).reshape(1024, 512)
    both[...] = mm(x2[...], w_high)
    up_low[...] = mm(x2[...], w_low[...])
    w_dn[...] = w_gu[:, 96:, :].reshape(768, 1024)
    grad_hidden[...] = mm_nt(cot[...], w_dn[...])
    for k in range(6):
        at = slice(128 * k, 128 * k + 128)
        gate = both[:, at]
        up = both[:, 768 + 128 * k : 896 + 128 * k] if k < 2 else up_low[:, 128 * k - 256 : 128 * k - 128]
        e = grad_hidden[:, at]
        sig = jax.nn.sigmoid(gate)
        hidden[:, at] = (gate * sig * up).astype(BF)
        grads[:, at] = (e * up * sig * (1.0 + gate * (1.0 - sig))).astype(BF)
        grads[:, 768 + 128 * k : 896 + 128 * k] = (e * gate * sig).astype(BF)
    partial = mm_nt(grads[:, :1024], w_high) + mm_nt(grads[:, 1024:], w_low[...])
    partial = partial.astype(BF)
    keep[:rows, :] = partial[:rows]
    send[:rows, :] = partial[rows : 2 * rows]
    keep[rows:, :] = partial[2 * rows : 3 * rows]
    send[rows:, :] = partial[3 * rows :]


def feed_forward_weights(x2, grads, hidden, cot, out):
    g = mm_tn(x2[...], grads[...]).astype(BF).reshape(8, 64, 1536)
    out[:, :64, :] = g[:, :, :1024]
    for k in range(4):
        low = g[:, :, 1024 + 128 * k : 1152 + 128 * k]
        out[:, 64:96, 256 * k : 256 * k + 128] = low[:, :32]
        out[:, 64:96, 256 * k + 128 : 256 * k + 256] = low[:, 32:]
    out[:, 96:, :] = mm_tn(hidden[...], cot[...]).astype(BF).reshape(8, 48, 1024)


def run_feed_forward(a, t, w_gu):
    tall, half = 576, 288
    return pl.pallas_call(
        feed_forward,
        out_shape=(
            whole((tall, 1024), BF),
            whole((tall, 1024), BF),
            whole((tall, 768), BF),
            whole((tall, 1536), BF),
            whole((half, 1024), BF),
            whole((half, 1024), BF),
            whole((768, 1024), BF),
        ),
        scratch_shapes=[
            pltpu.VMEM((1024, 512), BF),
            pltpu.VMEM((tall, 512), F32),
            pltpu.VMEM((tall, 1024), F32),
            pltpu.VMEM((tall, 768), F32),
        ],
        compiler_params=pltpu.CompilerParams(vmem_limit_bytes=56 << 20),
        cost_estimate=pl.CostEstimate(
            flops=4_600_000_000, transcendentals=450_000, bytes_accessed=16_000_000
        ),
        name="feed_forward",
    )(*a, *t, w_gu)


def run_feed_forward_weights(x2, grads, hidden, cot):
    tall = x2.shape[0]
    return pl.pallas_call(
        feed_forward_weights,
        grid=(2,),
        in_specs=[
            pl.BlockSpec((tall, 512), lambda k: (0, k)),
            pl.BlockSpec((tall, 1536), lambda k: (0, 0)),
            pl.BlockSpec((tall, 384), lambda k: (0, k)),
            pl.BlockSpec((tall, 1024), lambda k: (0, 0)),
        ],
        out_specs=pl.BlockSpec((8, 144, 1024), lambda k: (k, 0, 0)),
        out_shape=whole((NS, 144, 1024), BF),
        compiler_params=pltpu.CompilerParams(vmem_limit_bytes=56 << 20),
        cost_estimate=pl.CostEstimate(
            flops=2_700_000_000, transcendentals=0, bytes_accessed=10_000_000
        ),
        name="feed_forward_weights",
    )(x2, grads, hidden, cot)


def scatter_shard(a):
    return lax.all_to_all(a, SHARD, 0, 0).astype(F32).sum(0)


def core_swap(a):
    return lax.ppermute(a, "c", [(0, 1), (1, 0)])


def near_swap(a):
    return lax.ppermute(a, "z", [(0, 1), (1, 0), (2, 3), (3, 2)])


def far_swap(a):
    return lax.ppermute(a, "z", [(0, 3), (3, 0), (1, 2), (2, 1)])


def gather_four(a):
    far = near_swap(a)
    return [a, core_swap(a), far, core_swap(far)]


def scatter_four(keep, send):
    rows = keep.shape[0] // 2
    got = core_swap(send).astype(F32)
    pair = keep[rows:].astype(F32) + got[rows:]
    other = near_swap(pair.astype(BF))
    return keep[:rows].astype(F32) + got[:rows] + other.astype(F32)


def halves(partial, rows):
    block = lambda k: partial[k * rows : (k + 1) * rows]
    return (
        jnp.concatenate([block(0), block(2)], axis=0),
        jnp.concatenate([block(1), block(3)], axis=0),
    )


def after(a, *earlier):
    return lax.optimization_barrier((a,) + earlier)[0]


EVERY = ("y", "x", "z", "c")


def device(y, x, z, c):
    return ((y * 4 + x) * 4 + z) * 2 + c


def part_of(z, c):
    return (2 if z in (1, 2) else 0) + c


def column_heads(w_block):
    y, z, c = lax.axis_index("y"), lax.axis_index("z"), lax.axis_index("c")
    part = jnp.where((z == 1) | (z == 2), 2, 0) + c
    line = jnp.where(y == part, w_block, jnp.zeros_like(w_block))
    for k in (1, 2, 3):
        pairs = [
            (device(part_of(z, c), x, z, c), device((part_of(z, c) + k) % 4, x, z, c))
            for x in range(4)
            for z in range(4)
            for c in range(2)
        ]
        line = line + lax.ppermute(w_block, EVERY, pairs)
    return line


def line_heads(line):
    x = lax.axis_index("x")
    near = [line] + [
        lax.ppermute(line, "x", [(i, (i + k) % 4) for i in range(4)]) for k in (1, 2, 3)
    ]
    near = jnp.stack(near, axis=0)
    return jnp.concatenate(
        [lax.dynamic_index_in_dim(near, (x - h) % 4, 0, False) for h in range(4)], axis=0
    )


def local(
    tokens,
    positions,
    cotangent,
    attn_gain,
    w_query,
    key_projection,
    value_projection,
    q_gain,
    k_gain,
    w_output,
    ffn_gain,
    w_gate,
    w_up,
    w_down,
):
    z, core = lax.axis_index("z"), lax.axis_index("c")
    part = jnp.where((z == 1) | (z == 2), 2, 0) + core
    rows = tokens.shape[0]
    width = tokens.shape[1]
    head = 128
    tall = 4 * rows
    cut = lambda w, n: lax.dynamic_slice_in_dim(w, part * n, n, 1)
    cut_rows = lambda w, n: lax.dynamic_slice_in_dim(w, part * n, n, 0)

    member = 4 * lax.axis_index("y") + lax.axis_index("x")
    lane = lax.broadcasted_iota(jnp.int32, (16, width), 1)
    row = lax.broadcasted_iota(jnp.int32, (16, width), 0)
    again = lambda g: jnp.tile(g, (width // g.shape[0],))[None]
    q_lane = (lane // 8) == member
    k_lane = (lane // 8) == member + 16
    gain_rows = jnp.where(
        row < 2,
        jnp.where((lane // 64) == member, jnp.where(row == 0, again(attn_gain), again(ffn_gain)), 0),
        jnp.where(q_lane, again(q_gain), jnp.where(k_lane, again(k_gain), 0)),
    ).astype(BF)
    w_in = jnp.concatenate(
        [cut(w_query, 512), cut(key_projection, 256), cut(value_projection, 256)], axis=1
    )
    w_in = jnp.concatenate([w_in, gain_rows], axis=0)

    w_in = lax.all_gather(w_in, SHARD, axis=0)
    w_out = line_heads(column_heads(w_output))

    own = gather_four(jnp.concatenate([tokens, cotangent], axis=0))
    pos = jnp.stack(gather_four(positions), axis=0)
    x0 = jnp.concatenate([a[:rows] for a in own], axis=0)
    w_in, w_out, x0, pos = lax.optimization_barrier((w_in, w_out, x0, pos))

    source = lax.broadcasted_iota(jnp.int32, (1536, 384), 0)
    target = lax.broadcasted_iota(jnp.int32, (1536, 384), 1)
    chosen = (source == 192 * (target // 48) + 48 * part + target % 48).astype(BF)
    pick = lambda w: jnp.concatenate(
        [mm(w[:, :1536], chosen).astype(BF), mm(w[:, 1536:], chosen).astype(BF)], axis=1
    )
    gate_cut, up_cut = pick(w_gate), pick(w_up)
    low = up_cut[:, 256:]
    w_ff = jnp.concatenate(
        [
            jnp.concatenate([gate_cut, up_cut[:, :256]], axis=1),
            jnp.concatenate([low[:32], low[32:]], axis=1),
            cut_rows(w_down, 48),
        ],
        axis=0,
    )
    w_ff = lax.all_gather(after(w_ff, w_in), SHARD, axis=0)


    cosine, sine = rope_tables(pos.reshape(-1), head)
    cosine = jnp.concatenate([cosine, cosine], axis=-1)
    sine = jnp.concatenate([-sine, sine], axis=-1)
    stream_in = tokens.astype(F32)
    x1, raw, query, key, value, prob, att, w_in, gains = run_forward(
        w_in, x0, cosine, sine, pos.reshape(-1, 1)
    )
    norm_one, norm_two = gains[0], gains[1]
    scales = (gains[2:3, :128], gains[2:3, 128:256], cosine, sine)

    middle = stream_in + scatter_four(*halves(mm(att, w_out).astype(BF), rows))
    second_out, second_unit, second_factor = rms_forward(middle, norm_two)
    x2, cot, hidden, grads, keep, send, w_dn = run_feed_forward(
        gather_four(second_out.astype(BF)), own, w_ff
    )
    g_ff = run_feed_forward_weights(x2, grads, hidden, cot)
    g_ff_sum = lax.psum_scatter(g_ff, SHARD, scatter_dimension=0)
    grad_second = after(scatter_four(keep, send), g_ff)
    grad_part = rms_backward(grad_second, norm_two, second_unit, second_factor)
    grad_middle = cotangent.astype(F32) + grad_part
    gm = jnp.concatenate(gather_four(grad_middle.astype(BF)), axis=0)
    mixed = scatter_four(*halves(after(mm(hidden, w_dn).astype(BF), gm), rows))
    mixed = (middle + mixed).astype(BF)

    g_out = mm_tn(att, gm).astype(BF).reshape(4, NS, 8, width)
    g_out = jnp.transpose(g_out, (1, 0, 2, 3)).reshape(NS, 32, width)
    g_out_sum = lax.all_to_all(g_out, SHARD, 0, 0)
    grad_in, g_q, g_k = run_backward(after(gm, g_out), w_out, att, raw, query, key, value, prob, *scales)
    g_in = mm_tn(x1, grad_in).astype(BF).reshape(NS, 64, 1024)
    heads = jnp.concatenate(
        [g_q.reshape(NS, 1, 8), g_k.reshape(NS, 1, 8), jnp.zeros((NS, 1, width - 16), F32)], axis=2
    ).astype(BF)
    g_in = jnp.concatenate([g_in, heads, jnp.zeros((NS, 7, width), BF)], axis=1)
    grad_in = after(grad_in, g_in)
    grad_first = scatter_four(*halves(mm_nt(grad_in, w_in).astype(BF), rows))
    _, first_unit, first_factor = rms_forward(stream_in, norm_one)
    grad_part = rms_backward(grad_first, norm_one, first_unit, first_factor)
    grad_tokens = (grad_middle + grad_part).astype(BF)

    def finish(g):
        whole_g = jnp.stack(gather_four(g), axis=0)
        return [lax.dynamic_index_in_dim(whole_g, k ^ part, 0, False) for k in range(4)]

    pair = lambda g: (g + far_swap(g.astype(BF)).astype(F32)).astype(BF)
    g_out = finish(pair(g_out_sum.astype(F32).sum(0)))
    g_out = jnp.concatenate([g.reshape(4, 8, width) for g in g_out], axis=0)
    g_in_sum = lax.all_to_all(after(g_in, g_out_sum), SHARD, 0, 0)
    g_in = pair(g_in_sum.astype(F32).sum(0))
    g_ff = pair(g_ff_sum.astype(F32))
    g_out = lax.all_to_all(after(g_out, g_in), SHARD, 0, 0).reshape(128, width).astype(F32)
    g_in, g_ff = finish(g_in), finish(g_ff)
    heads = sum(g[64, :16].astype(F32) for g in g_in)
    side = lambda a, b: jnp.concatenate([g[:64, a:b].astype(F32) for g in g_in], axis=1)
    g_q, g_k, g_v = side(0, 512), side(512, 768), side(768, 1024)

    def hidden_order(pieces):
        source = lax.broadcasted_iota(jnp.int32, (1536, 1536), 0)
        target = lax.broadcasted_iota(jnp.int32, (1536, 1536), 1)
        at, k = target // 192, target % 192
        order = (source == 384 * (k // 48) + 48 * at + k % 48).astype(BF)
        half = lambda j: mm(
            jnp.concatenate([p[:, 384 * j : 384 * j + 384] for p in pieces], axis=1), order
        )
        return jnp.concatenate([half(0), half(1)], axis=1)

    halved = lambda g, k: jnp.concatenate(
        [g[64:96, 256 * k : 256 * k + 128], g[64:96, 256 * k + 128 : 256 * k + 256]], axis=0
    )
    lows = [jnp.concatenate([halved(g, k) for k in range(4)], axis=1) for g in g_ff]
    pieces = [
        jnp.concatenate([g[:64, :768], jnp.concatenate([g[:64, 768:], l], axis=1)], axis=0)
        for g, l in zip(g_ff, lows)
    ]
    g_gu = hidden_order(pieces)
    row = lambda w, g: jnp.sum(w.astype(F32) * g, axis=1)
    g_norm_one = row(w_query, g_q) + row(key_projection, g_k) + row(value_projection, g_v)
    g_norm_two = row(w_gate, g_gu[:64]) + row(w_up, g_gu[64:])
    return (
        mixed,
        grad_tokens,
        g_norm_one / attn_gain.astype(F32),
        g_q,
        g_k,
        g_v,
        heads[:8],
        heads[8:],
        g_out,
        g_norm_two / ffn_gain.astype(F32),
        g_gu[:64],
        g_gu[64:],
        jnp.concatenate([g[96:].astype(F32) for g in g_ff], axis=0),
    )


def solution(mesh):
    fine = Mesh(mesh.devices.reshape(4, 4, 4, 2), ("y", "x", "z", "c"))
    every = ("y", "x", "z", "c")
    shard1 = P(SHARD)
    shard2 = P(SHARD, None)
    return jax.shard_map(
        local,
        mesh=fine,
        in_specs=(
            P(every, None), P(every), P(every, None), shard1, shard2, shard2, shard2,
            shard1, shard1, shard2, shard1, shard2, shard2, shard2,
        ),
        out_specs=(
            P(every, None), P(every, None), shard1, shard2, shard2, shard2,
            shard1, shard1, shard2, shard1, shard2, shard2, shard2,
        ),
        check_vma=False,
    )
```

```python
import math

import jax
import jax.numpy as jnp
from jax import lax
from jax.experimental import pallas as pl
from jax.experimental.pallas import tpu as pltpu
from jax.sharding import Mesh, PartitionSpec as P

EPSILON = 1e-06
THETA = 1000000.0
SHARD = ("y", "x")
NS = 16
BF = jnp.bfloat16
F32 = jnp.float32


def rms_forward(inputs, scales):
    factor = lax.rsqrt(jnp.mean(inputs * inputs, axis=-1, keepdims=True) + EPSILON)
    normed = inputs * factor
    return (normed * scales, normed, factor)


def rms_backward(grad_out, scales, normed, factor):
    grad_normed = grad_out * scales
    return factor * (
        grad_normed - normed * jnp.mean(grad_normed * normed, axis=-1, keepdims=True)
    )


def rope_tables(positions, head_dim):
    half_dim = head_dim // 2
    frequency = jnp.exp(
        jnp.arange(half_dim).astype(F32) * (-2.0 * math.log(THETA) / head_dim)
    )
    angles = positions.astype(F32)[..., None] * frequency
    return (jnp.cos(angles), jnp.sin(angles))


def mm(left, right):
    return jnp.dot(left, right, preferred_element_type=F32)


def mm_nt(left, right):
    return lax.dot_general(left, right, (((1,), (1,)), ((), ())), preferred_element_type=F32)


def mm_tn(left, right):
    return lax.dot_general(left, right, (((0,), (0,)), ((), ())), preferred_element_type=F32)


def whole(shape, dtype):
    return jax.ShapeDtypeStruct(shape, dtype)


def turned(a, cosine, sine):
    return a * cosine + pltpu.roll(a, 64, axis=1) * sine


def attention_forward(
    w_all, x0, cosine, sine, position,
    x1, raw, query, key, value, prob, att, w_in, gains,
):
    rows = 144
    w_in[...] = w_all[:, :64, :].reshape(1024, 1024)
    gains[...] = w_all[:, 64:, :].astype(F32).sum(0)
    norm_one = gains[0:1, :]
    q_scale, k_scale = gains[2:3, :128], gains[2:3, 128:256]
    stream = x0[...].astype(F32)
    factor = lax.rsqrt(jnp.mean(stream * stream, axis=-1, keepdims=True) + EPSILON)
    x1[...] = (stream * factor * norm_one).astype(BF)
    cos, sin = cosine[...], sine[...]
    for h in range(8):
        at = slice(128 * h, 128 * h + 128)
        if h % 2 == 0:
            two = mm(x1[...], w_in[:, 128 * h : 128 * h + 256])
        part = two[:, 128 * (h % 2) : 128 * (h % 2) + 128]
        if h < 6:
            raw[:, at] = part
            scale = q_scale if h < 4 else k_scale
            factor = lax.rsqrt(jnp.mean(part * part, axis=-1, keepdims=True) + EPSILON)
            done = turned(part * factor * scale, cos, sin).astype(BF)
            if h < 4:
                query[:, at] = done
            else:
                key[:, 128 * (h - 4) : 128 * (h - 4) + 128] = done
        else:
            value[:, 128 * (h - 6) : 128 * (h - 6) + 128] = part.astype(BF)
    near = lax.broadcasted_iota(jnp.int32, (rows, rows), 1)
    this = lax.broadcasted_iota(jnp.int32, (rows, rows), 0)
    for b in range(4):
        own = slice(rows * b, rows * b + rows)
        allowed = (near <= this) & (near >= this - position[own, :])
        allowed = jnp.concatenate([allowed.astype(F32)] * 2, axis=0) > 0.5
        for j in range(2):
            kv = slice(128 * j, 128 * j + 128)
            one = slice(256 * j, 256 * j + 128)
            two = slice(256 * j + 128, 256 * j + 256)
            q = jnp.concatenate([query[own, one], query[own, two]], axis=0)
            scores = jnp.where(allowed, mm_nt(q, key[own, kv]) * 128 ** (-0.5), -1e30)
            weights = jnp.exp(scores - jnp.max(scores, axis=-1, keepdims=True))
            p = weights / jnp.sum(weights, axis=-1, keepdims=True)
            prob[2 * b + j] = p
            out = mm(p.astype(BF), value[own, kv]).astype(BF)
            att[own, one] = out[:rows]
            att[own, two] = out[rows:]


def attention_backward(
    gm, w_out, att, raw, query, key, value, prob, q_scale, k_scale, cosine, sine,
    grad_in, g_q, g_k, grad_att, d_query, d_key,
):
    rows = 144
    grad_att[...] = mm_nt(gm[...], w_out[...]).astype(BF)
    for b in range(4):
        own = slice(rows * b, rows * b + rows)
        for j in range(2):
            kv = slice(128 * j, 128 * j + 128)
            one = slice(256 * j, 256 * j + 128)
            two = slice(256 * j + 128, 256 * j + 256)
            both = lambda ref: jnp.concatenate([ref[own, one], ref[own, two]], axis=0)
            p = prob[2 * b + j]
            d_out = both(grad_att)
            grad_in[own, 768 + 128 * j : 896 + 128 * j] = mm_tn(p.astype(BF), d_out).astype(BF)
            d_prob = mm_nt(d_out, value[own, kv])
            delta = jnp.sum(
                d_out.astype(F32) * both(att).astype(F32), axis=-1, keepdims=True
            )
            d_scores = (p * (d_prob - delta) * 128 ** (-0.5)).astype(BF)
            d_q = mm(d_scores, key[own, kv])
            d_query[own, one] = d_q[:rows]
            d_query[own, two] = d_q[rows:]
            d_key[own, kv] = mm_tn(d_scores, both(query))
    cos, sin = cosine[...], sine[...]
    for h in range(6):
        at = slice(128 * h, 128 * h + 128)
        part = raw[:, at]
        factor = lax.rsqrt(jnp.mean(part * part, axis=-1, keepdims=True) + EPSILON)
        unit = part * factor
        if h < 4:
            e, scale, total_ref = d_query[:, at], q_scale[...], g_q
        else:
            e, scale, total_ref = d_key[:, 128 * (h - 4) : 128 * (h - 4) + 128], k_scale[...], g_k
        e = turned(e, cos, -sin)
        line = jnp.sum(e * unit, axis=0, keepdims=True)
        total_ref[...] = line if h in (0, 4) else total_ref[...] + line
        e = e * scale
        grad_in[:, at] = (
            factor * (e - unit * jnp.mean(e * unit, axis=-1, keepdims=True))
        ).astype(BF)


def run_forward(w_all, x0, cosine, sine, position):
    tall = x0.shape[0]
    return pl.pallas_call(
        attention_forward,
        out_shape=(
            whole((tall, 1024), BF),
            whole((tall, 768), F32),
            whole((tall, 512), BF),
            whole((tall, 256), BF),
            whole((tall, 256), BF),
            whole((8, 288, 144), F32),
            whole((tall, 512), BF),
            whole((1024, 1024), BF),
            whole((16, 1024), F32),
        ),
        compiler_params=pltpu.CompilerParams(vmem_limit_bytes=56 << 20),
        cost_estimate=pl.CostEstimate(
            flops=1_600_000_000, transcendentals=400_000, bytes_accessed=12_000_000
        ),
        name="attention_forward",
    )(w_all, x0, cosine, sine, position)


def run_backward(gm, w_out, att, raw, query, key, value, prob, q_scale, k_scale, cosine, sine):
    tall = gm.shape[0]
    return pl.pallas_call(
        attention_backward,
        out_shape=(
            whole((tall, 1024), BF),
            whole((1, 128), F32),
            whole((1, 128), F32),
        ),
        scratch_shapes=[
            pltpu.VMEM((tall, 512), BF),
            pltpu.VMEM((tall, 512), F32),
            pltpu.VMEM((tall, 256), F32),
        ],
        compiler_params=pltpu.CompilerParams(vmem_limit_bytes=56 << 20),
        cost_estimate=pl.CostEstimate(
            flops=1_200_000_000, transcendentals=4_000, bytes_accessed=12_000_000
        ),
        name="attention_backward",
    )(gm, w_out, att, raw, query, key, value, prob, q_scale, k_scale, cosine, sine)


def feed_forward(
    a0, a1, a2, a3, t0, t1, t2, t3, w_gu,
    x2, cot, hidden, grads, keep, send, w_dn, w_low, up_low, both, grad_hidden,
):
    rows = 144
    for k, (a, t) in enumerate(((a0, t0), (a1, t1), (a2, t2), (a3, t3))):
        x2[rows * k : rows * k + rows, :] = a[...]
        cot[rows * k : rows * k + rows, :] = t[rows:, :]
    w_high = w_gu[:, :64, :].reshape(1024, 1024)
    w_low[...] = jnp.concatenate(
        [w_gu[:, 64:96, :512], w_gu[:, 64:96, 512:]], axis=1
    ).reshape(1024, 512)
    both[...] = mm(x2[...], w_high)
    up_low[...] = mm(x2[...], w_low[...])
    w_dn[...] = w_gu[:, 96:, :].reshape(768, 1024)
    grad_hidden[...] = mm_nt(cot[...], w_dn[...])
    for k in range(6):
        at = slice(128 * k, 128 * k + 128)
        gate = both[:, at]
        up = both[:, 768 + 128 * k : 896 + 128 * k] if k < 2 else up_low[:, 128 * k - 256 : 128 * k - 128]
        e = grad_hidden[:, at]
        sig = jax.nn.sigmoid(gate)
        hidden[:, at] = (gate * sig * up).astype(BF)
        grads[:, at] = (e * up * sig * (1.0 + gate * (1.0 - sig))).astype(BF)
        grads[:, 768 + 128 * k : 896 + 128 * k] = (e * gate * sig).astype(BF)
    partial = mm_nt(grads[:, :1024], w_high) + mm_nt(grads[:, 1024:], w_low[...])
    partial = partial.astype(BF)
    keep[:rows, :] = partial[:rows]
    send[:rows, :] = partial[rows : 2 * rows]
    keep[rows:, :] = partial[2 * rows : 3 * rows]
    send[rows:, :] = partial[3 * rows :]


def feed_forward_weights(x2, grads, hidden, cot, out):
    g = mm_tn(x2[...], grads[...]).astype(BF).reshape(8, 64, 1536)
    out[:, :64, :] = g[:, :, :1024]
    for k in range(4):
        low = g[:, :, 1024 + 128 * k : 1152 + 128 * k]
        out[:, 64:96, 256 * k : 256 * k + 128] = low[:, :32]
        out[:, 64:96, 256 * k + 128 : 256 * k + 256] = low[:, 32:]
    out[:, 96:, :] = mm_tn(hidden[...], cot[...]).astype(BF).reshape(8, 48, 1024)


def run_feed_forward(a, t, w_gu):
    tall, half = 576, 288
    return pl.pallas_call(
        feed_forward,
        out_shape=(
            whole((tall, 1024), BF),
            whole((tall, 1024), BF),
            whole((tall, 768), BF),
            whole((tall, 1536), BF),
            whole((half, 1024), BF),
            whole((half, 1024), BF),
            whole((768, 1024), BF),
        ),
        scratch_shapes=[
            pltpu.VMEM((1024, 512), BF),
            pltpu.VMEM((tall, 512), F32),
            pltpu.VMEM((tall, 1024), F32),
            pltpu.VMEM((tall, 768), F32),
        ],
        compiler_params=pltpu.CompilerParams(vmem_limit_bytes=56 << 20),
        cost_estimate=pl.CostEstimate(
            flops=4_600_000_000, transcendentals=450_000, bytes_accessed=16_000_000
        ),
        name="feed_forward",
    )(*a, *t, w_gu)


def run_feed_forward_weights(x2, grads, hidden, cot):
    tall = x2.shape[0]
    return pl.pallas_call(
        feed_forward_weights,
        grid=(2,),
        in_specs=[
            pl.BlockSpec((tall, 512), lambda k: (0, k)),
            pl.BlockSpec((tall, 1536), lambda k: (0, 0)),
            pl.BlockSpec((tall, 384), lambda k: (0, k)),
            pl.BlockSpec((tall, 1024), lambda k: (0, 0)),
        ],
        out_specs=pl.BlockSpec((8, 144, 1024), lambda k: (k, 0, 0)),
        out_shape=whole((NS, 144, 1024), BF),
        compiler_params=pltpu.CompilerParams(vmem_limit_bytes=56 << 20),
        cost_estimate=pl.CostEstimate(
            flops=2_700_000_000, transcendentals=0, bytes_accessed=10_000_000
        ),
        name="feed_forward_weights",
    )(x2, grads, hidden, cot)


def scatter_shard(a):
    return lax.all_to_all(a, SHARD, 0, 0).astype(F32).sum(0)


def core_swap(a):
    return lax.ppermute(a, "c", [(0, 1), (1, 0)])


def near_swap(a):
    return lax.ppermute(a, "z", [(0, 1), (1, 0), (2, 3), (3, 2)])


def far_swap(a):
    return lax.ppermute(a, "z", [(0, 3), (3, 0), (1, 2), (2, 1)])


def gather_four(a):
    far = near_swap(a)
    return [a, core_swap(a), far, core_swap(far)]


def scatter_four(keep, send):
    rows = keep.shape[0] // 2
    got = core_swap(send).astype(F32)
    pair = keep[rows:].astype(F32) + got[rows:]
    other = near_swap(pair.astype(BF))
    return keep[:rows].astype(F32) + got[:rows] + other.astype(F32)


def halves(partial, rows):
    block = lambda k: partial[k * rows : (k + 1) * rows]
    return (
        jnp.concatenate([block(0), block(2)], axis=0),
        jnp.concatenate([block(1), block(3)], axis=0),
    )


def after(a, *earlier):
    return lax.optimization_barrier((a,) + earlier)[0]


EVERY = ("y", "x", "z", "c")


def device(y, x, z, c):
    return ((y * 4 + x) * 4 + z) * 2 + c


def part_of(z, c):
    return (2 if z in (1, 2) else 0) + c


def column_heads(w_block):
    y, z, c = lax.axis_index("y"), lax.axis_index("z"), lax.axis_index("c")
    part = jnp.where((z == 1) | (z == 2), 2, 0) + c
    line = jnp.where(y == part, w_block, jnp.zeros_like(w_block))
    for k in (1, 2, 3):
        pairs = [
            (device(part_of(z, c), x, z, c), device((part_of(z, c) + k) % 4, x, z, c))
            for x in range(4)
            for z in range(4)
            for c in range(2)
        ]
        line = line + lax.ppermute(w_block, EVERY, pairs)
    return line


def line_heads(line):
    x = lax.axis_index("x")
    near = [line] + [
        lax.ppermute(line, "x", [(i, (i + k) % 4) for i in range(4)]) for k in (1, 2, 3)
    ]
    near = jnp.stack(near, axis=0)
    return jnp.concatenate(
        [lax.dynamic_index_in_dim(near, (x - h) % 4, 0, False) for h in range(4)], axis=0
    )


def local(
    tokens,
    positions,
    cotangent,
    attn_gain,
    w_query,
    key_projection,
    value_projection,
    q_gain,
    k_gain,
    w_output,
    ffn_gain,
    w_gate,
    w_up,
    w_down,
):
    z, core = lax.axis_index("z"), lax.axis_index("c")
    part = jnp.where((z == 1) | (z == 2), 2, 0) + core
    rows = tokens.shape[0]
    width = tokens.shape[1]
    head = 128
    tall = 4 * rows
    cut = lambda w, n: lax.dynamic_slice_in_dim(w, part * n, n, 1)
    cut_rows = lambda w, n: lax.dynamic_slice_in_dim(w, part * n, n, 0)

    member = 4 * lax.axis_index("y") + lax.axis_index("x")
    lane = lax.broadcasted_iota(jnp.int32, (16, width), 1)
    row = lax.broadcasted_iota(jnp.int32, (16, width), 0)
    again = lambda g: jnp.tile(g, (width // g.shape[0],))[None]
    q_lane = (lane // 8) == member
    k_lane = (lane // 8) == member + 16
    gain_rows = jnp.where(
        row < 2,
        jnp.where((lane // 64) == member, jnp.where(row == 0, again(attn_gain), again(ffn_gain)), 0),
        jnp.where(q_lane, again(q_gain), jnp.where(k_lane, again(k_gain), 0)),
    ).astype(BF)
    w_in = jnp.concatenate(
        [cut(w_query, 512), cut(key_projection, 256), cut(value_projection, 256)], axis=1
    )
    w_in = jnp.concatenate([w_in, gain_rows], axis=0)

    w_in = lax.all_gather(w_in, SHARD, axis=0)
    w_out = line_heads(column_heads(w_output))

    own = gather_four(jnp.concatenate([tokens, cotangent], axis=0))
    pos = jnp.stack(gather_four(positions), axis=0)
    x0 = jnp.concatenate([a[:rows] for a in own], axis=0)
    w_in, w_out, x0, pos = lax.optimization_barrier((w_in, w_out, x0, pos))

    source = lax.broadcasted_iota(jnp.int32, (1536, 384), 0)
    target = lax.broadcasted_iota(jnp.int32, (1536, 384), 1)
    chosen = (source == 192 * (target // 48) + 48 * part + target % 48).astype(BF)
    pick = lambda w: jnp.concatenate(
        [mm(w[:, :1536], chosen).astype(BF), mm(w[:, 1536:], chosen).astype(BF)], axis=1
    )
    gate_cut, up_cut = pick(w_gate), pick(w_up)
    low = up_cut[:, 256:]
    w_ff = jnp.concatenate(
        [
            jnp.concatenate([gate_cut, up_cut[:, :256]], axis=1),
            jnp.concatenate([low[:32], low[32:]], axis=1),
            cut_rows(w_down, 48),
        ],
        axis=0,
    )
    w_ff = lax.all_gather(after(w_ff, w_in), SHARD, axis=0)


    cosine, sine = rope_tables(pos.reshape(-1), head)
    cosine = jnp.concatenate([cosine, cosine], axis=-1)
    sine = jnp.concatenate([-sine, sine], axis=-1)
    stream_in = tokens.astype(F32)
    x1, raw, query, key, value, prob, att, w_in, gains = run_forward(
        w_in, x0, cosine, sine, pos.reshape(-1, 1)
    )
    norm_one, norm_two = gains[0], gains[1]
    scales = (gains[2:3, :128], gains[2:3, 128:256], cosine, sine)

    middle = stream_in + scatter_four(*halves(mm(att, w_out).astype(BF), rows))
    second_out, second_unit, second_factor = rms_forward(middle, norm_two)
    x2, cot, hidden, grads, keep, send, w_dn = run_feed_forward(
        gather_four(second_out.astype(BF)), own, w_ff
    )
    g_ff = run_feed_forward_weights(x2, grads, hidden, cot)
    g_ff_sum = lax.psum_scatter(g_ff, SHARD, scatter_dimension=0)
    grad_second = after(scatter_four(keep, send), g_ff)
    grad_part = rms_backward(grad_second, norm_two, second_unit, second_factor)
    grad_middle = cotangent.astype(F32) + grad_part
    gm = jnp.concatenate(gather_four(grad_middle.astype(BF)), axis=0)
    mixed = scatter_four(*halves(after(mm(hidden, w_dn).astype(BF), gm), rows))
    mixed = (middle + mixed).astype(BF)

    g_out = mm_tn(att, gm).astype(BF).reshape(4, NS, 8, width)
    g_out = jnp.transpose(g_out, (1, 0, 2, 3)).reshape(NS, 32, width)
    g_out_sum = lax.all_to_all(g_out, SHARD, 0, 0)
    grad_in, g_q, g_k = run_backward(after(gm, g_out), w_out, att, raw, query, key, value, prob, *scales)
    g_in = mm_tn(x1, grad_in).astype(BF).reshape(NS, 64, 1024)
    heads = jnp.concatenate(
        [g_q.reshape(NS, 1, 8), g_k.reshape(NS, 1, 8), jnp.zeros((NS, 1, width - 16), F32)], axis=2
    ).astype(BF)
    g_in = jnp.concatenate([g_in, heads, jnp.zeros((NS, 7, width), BF)], axis=1)
    grad_in = after(grad_in, g_in)
    grad_first = scatter_four(*halves(mm_nt(grad_in, w_in).astype(BF), rows))
    _, first_unit, first_factor = rms_forward(stream_in, norm_one)
    grad_part = rms_backward(grad_first, norm_one, first_unit, first_factor)
    grad_tokens = (grad_middle + grad_part).astype(BF)

    def finish(g):
        whole_g = jnp.stack(gather_four(g), axis=0)
        return [lax.dynamic_index_in_dim(whole_g, k ^ part, 0, False) for k in range(4)]

    pair = lambda g: (g + far_swap(g.astype(BF)).astype(F32)).astype(BF)
    g_out = finish(pair(g_out_sum.astype(F32).sum(0)))
    g_out = jnp.concatenate([g.reshape(4, 8, width) for g in g_out], axis=0)
    g_in_sum = lax.all_to_all(after(g_in, g_out_sum), SHARD, 0, 0)
    g_in = pair(g_in_sum.astype(F32).sum(0))
    g_ff = pair(g_ff_sum.astype(F32))
    g_out = lax.all_to_all(after(g_out, g_in, g_ff), SHARD, 0, 0).reshape(128, width).astype(F32)
    g_in, g_ff = finish(g_in), finish(g_ff)
    heads = sum(g[64, :16].astype(F32) for g in g_in)
    side = lambda a, b: jnp.concatenate([g[:64, a:b].astype(F32) for g in g_in], axis=1)
    g_q, g_k, g_v = side(0, 512), side(512, 768), side(768, 1024)

    def hidden_order(pieces):
        source = lax.broadcasted_iota(jnp.int32, (1536, 1536), 0)
        target = lax.broadcasted_iota(jnp.int32, (1536, 1536), 1)
        at, k = target // 192, target % 192
        order = (source == 384 * (k // 48) + 48 * at + k % 48).astype(BF)
        half = lambda j: mm(
            jnp.concatenate([p[:, 384 * j : 384 * j + 384] for p in pieces], axis=1), order
        )
        return jnp.concatenate([half(0), half(1)], axis=1)

    halved = lambda g, k: jnp.concatenate(
        [g[64:96, 256 * k : 256 * k + 128], g[64:96, 256 * k + 128 : 256 * k + 256]], axis=0
    )
    lows = [jnp.concatenate([halved(g, k) for k in range(4)], axis=1) for g in g_ff]
    pieces = [
        jnp.concatenate([g[:64, :768], jnp.concatenate([g[:64, 768:], l], axis=1)], axis=0)
        for g, l in zip(g_ff, lows)
    ]
    g_gu = hidden_order(pieces)
    row = lambda w, g: jnp.sum(w.astype(F32) * g, axis=1)
    g_norm_one = row(w_query, g_q) + row(key_projection, g_k) + row(value_projection, g_v)
    g_norm_two = row(w_gate, g_gu[:64]) + row(w_up, g_gu[64:])
    return (
        mixed,
        grad_tokens,
        g_norm_one / attn_gain.astype(F32),
        g_q,
        g_k,
        g_v,
        heads[:8],
        heads[8:],
        g_out,
        g_norm_two / ffn_gain.astype(F32),
        g_gu[:64],
        g_gu[64:],
        jnp.concatenate([g[96:].astype(F32) for g in g_ff], axis=0),
    )


def solution(mesh):
    fine = Mesh(mesh.devices.reshape(4, 4, 4, 2), ("y", "x", "z", "c"))
    every = ("y", "x", "z", "c")
    shard1 = P(SHARD)
    shard2 = P(SHARD, None)
    return jax.shard_map(
        local,
        mesh=fine,
        in_specs=(
            P(every, None), P(every), P(every, None), shard1, shard2, shard2, shard2,
            shard1, shard1, shard2, shard1, shard2, shard2, shard2,
        ),
        out_specs=(
            P(every, None), P(every, None), shard1, shard2, shard2, shard2,
            shard1, shard1, shard2, shard1, shard2, shard2, shard2,
        ),
        check_vma=False,
    )
```
